32 devices in a mesh: horiz: 8 (over z, y), rad: 4 (over x, core).
Axes of the slice: x: 2, y: 2, z: 4, core: 2. Of those that a mesh axis runs over, the one named last changes fastest.
Arguments:
- field_state: bfloat16 [64, 512, 256], P('horiz', 'rad'), may hold values from -6 to 6
- deriv_pair: bfloat16 [64, 128], replicated, may hold values from -0.75 to 0.75
- face_blocks: bfloat16 [32, 64], replicated, may hold values from -1 to 1
- interp_blocks: bfloat16 [16, 64, 64], replicated, may hold values from -0.5 to 0.5
- radial_ops: bfloat16 [4, 512, 512], replicated, may hold values from -0.25 to 0.25
- neighbours: int32 [64, 4], P('horiz'), may hold values from 0 to 63, as said below
- donor_ids: int32 [64, 2], P('horiz'), may hold values from 0 to 63, as said below
- donor_mats: int32 [64, 2], P('horiz'), may hold values from 0 to 15
Outputs:
- new_state: bfloat16 [64, 512, 256], P('horiz', 'rad')
The draws below stay inside these ranges and needn't reach their ends.
Inputs may be any that keep to these rules, and one draw needn't show every extreme that they name: `neighbours`: slots 0 and 1 of element e hold e - 1 and e + 1; slot 2 holds e - 1 - a and slot 3 holds e + 1 + b with a and b from 0 to 1; all modulo 64. `donor_ids`: the donors of element e lie in the block of 8 elements that starts at ((e // 8) * 8 + 64 // 2) modulo 64.
All inputs are finite; a program needn't handle non-finite values.
Results may differ from the reference program's by a relative error of at most 0.0049.
Values may be sent and summed in bfloat16 or wider, within the bound.
A program may use at most 64 MiB of HBM per device.

```python
import jax
import jax.numpy as jnp
import numpy as np
from jax import lax

SIDE = 8
NODE = 64
NF = 4
NR = 512
NMAT = 16
NDON = 2
HALO = 2
E_DEV = 8
ELEMENTS = 64


def draw_neighbours(key, part):
    element = jnp.arange(ELEMENTS, dtype=jnp.int32)
    key_low, key_high = jax.random.split(key)
    low_step = jax.random.randint(key_low, (ELEMENTS,), 0, HALO, dtype=jnp.int32)
    high_step = jax.random.randint(key_high, (ELEMENTS,), 0, HALO, dtype=jnp.int32)
    listing = jnp.stack([element - 1, element + 1, element - 1 - low_step, element + 1 + high_step], axis=1)
    return jnp.mod(listing, ELEMENTS).astype(jnp.int32)


def draw_donor_ids(key, part):
    element = jnp.arange(ELEMENTS, dtype=jnp.int32)
    block_start = jnp.mod(element // E_DEV * E_DEV + ELEMENTS // 2, ELEMENTS)
    offsets = jax.random.randint(key, (ELEMENTS, NDON), 0, E_DEV, dtype=jnp.int32)
    return (block_start[:, None] + offsets).astype(jnp.int32)


def set_ends(entries, key, smallest, high):
    index_at = [jax.random.randint(jax.random.fold_in(key, axis), (), 0, length) for axis, length in enumerate(entries.shape)]
    widest = entries.shape.index(max(entries.shape))
    neighbour = index_at[:widest] + [(index_at[widest] + 1) % entries.shape[widest]] + index_at[widest + 1:]
    return entries.at[tuple(index_at)].set(smallest).at[tuple(neighbour)].set(high)


def shard_levels(key, shape, shards, least, high):
    level = 1.0
    for dim, parts in shards:
        steps = jax.random.uniform(jax.random.fold_in(jax.random.fold_in(key, 6), dim), (parts,), jnp.float32, least / len(shards), high / len(shards))
        level = level * jnp.repeat(jnp.exp(steps), shape[dim] // parts).reshape((-1,) + (1,) * (len(shape) - 1 - dim))
    return level


def normal_values(own_key, extent, scale, limit, pieces=(), kind=jnp.bfloat16):
    values = jax.random.normal(own_key, extent, jnp.float32) * scale
    if len(pieces) > 0:
        values = shard_levels(own_key, extent, pieces, -0.22, 0.18) * values
    return jnp.clip(values, min=-limit, max=limit).astype(kind)


def setup_inputs(seed: int = 0) -> dict:
    key_of = jax.random.split(jax.random.key(seed), 9)
    field_state = normal_values(key_of[0], (ELEMENTS, NR, NF * NODE), 1.0, 6.0, ((0, 8), (1, 4)))
    deriv_pair = normal_values(key_of[1], (NODE, 2 * NODE), NODE ** -0.5, 0.75)
    face_blocks = normal_values(key_of[2], (4 * SIDE, NODE), (4 * SIDE) ** -0.5, 1.0)
    interp_blocks = normal_values(key_of[3], (NMAT, NODE, NODE), (NDON * NODE) ** -0.5, 0.5)
    radial_ops = normal_values(key_of[4], (NF, NR, NR), NR ** -0.5, 0.25)
    neighbours = draw_neighbours(jax.random.fold_in(key_of[8], 71), 0)
    donor_ids = draw_donor_ids(jax.random.fold_in(key_of[8], 71), 0)
    donor_mats = set_ends(jax.random.randint(key_of[7], (ELEMENTS, NDON), 0, NMAT), jax.random.fold_in(key_of[7], 1), 0, NMAT - 1).astype(jnp.int32)
    return dict(field_state=field_state, deriv_pair=deriv_pair, face_blocks=face_blocks, interp_blocks=interp_blocks, radial_ops=radial_ops, neighbours=neighbours, donor_ids=donor_ids, donor_mats=donor_mats)


def edge_index_table(side):
    steps = np.arange(side)
    return np.stack([(side - 1) * side + steps, steps, steps * side + side - 1, steps * side]).reshape(-1)


def reference(field_state, deriv_pair, face_blocks, interp_blocks, radial_ops, neighbours, donor_ids, donor_mats):
    edge_index = edge_index_table(SIDE)
    state_four = field_state.reshape(ELEMENTS, NR, NF, NODE)
    edge_vals = state_four[:, :, :, edge_index]
    deriv_full = deriv_pair.astype(jnp.float32)
    face_full = face_blocks.astype(jnp.float32)
    radial_full = radial_ops.astype(jnp.float32)

    def block_step(block):
        begin_at = (block * E_DEV).astype(jnp.int32)
        own_vals = lax.dynamic_slice_in_dim(state_four, begin_at, E_DEV, 0).astype(jnp.float32)
        near_ids = lax.dynamic_slice_in_dim(neighbours, begin_at, E_DEV, 0)
        nbr_rows = edge_vals[near_ids].reshape(E_DEV, 4, NR, NF, 4, SIDE)
        facing = jnp.stack([nbr_rows[:, slot, :, :, slot, :] for slot in range(4)], axis=3)
        facing = facing.reshape(E_DEV, NR, NF, 4 * SIDE).astype(jnp.float32)
        couple = jnp.einsum("erfk,km->erfm", facing, face_full)
        gradients = jnp.einsum("erfn,nm->erfm", own_vals, deriv_full)
        grad_x = gradients[..., :NODE]
        grad_y = gradients[..., NODE:]
        flux_term = own_vals[:, :, 0:1, :] * grad_x + own_vals[:, :, 1:2, :] * grad_y
        don_ids = lax.dynamic_slice_in_dim(donor_ids, begin_at, E_DEV, 0)
        mat_ids = lax.dynamic_slice_in_dim(donor_mats, begin_at, E_DEV, 0)
        don_rows = state_four[don_ids].astype(jnp.float32)
        matrices = interp_blocks[mat_ids].astype(jnp.float32)
        donor_sum = jnp.einsum("ejrfn,ejnm->erfm", don_rows, matrices)
        sectioned = (own_vals + couple + donor_sum - flux_term).astype(jnp.bfloat16)
        result = jnp.einsum("frs,esfn->erfn", radial_full, sectioned.astype(jnp.float32))
        return result.astype(jnp.bfloat16)

    blocks = lax.map(block_step, jnp.arange(ELEMENTS // E_DEV, dtype=jnp.int32))
    return blocks.reshape(ELEMENTS, NR, NF * NODE)
```

```python
import functools

import jax
import jax.numpy as jnp
from jax import lax
from jax.experimental import pallas as pl
from jax.experimental.pallas import tpu as pltpu
from jax.sharding import PartitionSpec as P

SIDE = 8
HALO = 2
MESH = pl.DeviceIdType.MESH
BF = jnp.bfloat16
F32 = jnp.float32


def dot(a, b):
    return jnp.dot(a, b, preferred_element_type=F32)


def iota(shape, dim):
    return lax.broadcasted_iota(jnp.int32, shape, dim)


def onehot(mask):
    return jnp.where(mask, 1.0, 0.0).astype(BF)


def rim_position(lane, node, side, above, far):
    field, n = lane // node, lane % node
    i, j = n // side, n % side
    last = 0 if above else side - 1
    base = field * (node // 2)
    if far:
        return jnp.where(j == last, base + 2 * side + i, -1)
    return jnp.where(i == last, base + j, jnp.where(j == last, base + side + i, -1))


def kernel(
    dims,
    field, deriv_in, face_in, interp_in, radial, nbr_in, don_id_in, don_mat_in,
    out,
    ext, rows, pack, got, grad_w, face_w, blocks,
    gat_u, gat_s, gat_a, local01, acc23, vbuf, don01, don23,
    nbr, don_id, don_mat, deriv, face, interp,
    local_sem, rim_sem, don_sem, send_sem, far_sem, near_sem, ready,
):
    horiz, rad, elem, rdev, nf, node, nmat, ndon = dims
    width = nf * node
    pair = 2 * node
    half = width - pair
    order = rad * rdev
    chips = rad // 2
    h, me = lax.axis_index("horiz"), lax.axis_index("rad")
    elements = elem * horiz
    first = h * elem
    up, down = lax.rem(h + 1, horiz), lax.rem(h + horiz - 1, horiz)
    across = lax.rem(h + horiz // 2, horiz)
    second = lax.rem(me, 2)
    core = me + 1 - 2 * second
    base = me - second
    quarter = horiz // 4
    outer = (h < quarter) | (h >= horiz - quarter)
    inner = jnp.logical_not(outer)
    own = ext.at[pl.ds(HALO, elem)]

    load_field = pltpu.make_async_copy(field, own, local_sem.at[0])
    load_rows = pltpu.make_async_copy(
        radial.at[:, pl.ds(pl.multiple_of(me * rdev, rdev), rdev), :], rows, local_sem.at[1]
    )
    load_field.start()
    load_small = [pltpu.make_async_copy(a, b, local_sem.at[2 + i]) for i, (a, b) in enumerate(
        ((deriv_in, deriv), (face_in, face), (interp_in, interp),
         (nbr_in, nbr), (don_id_in, don_id), (don_mat_in, don_mat)))]
    for cp in load_small:
        cp.start()
    load_rows.start()

    barrier = pltpu.get_barrier_semaphore()
    peers = [(up, me), (down, me), (across, me), (h, core)]
    peers += [(h, lax.rem(me + 2 * t, rad)) for t in range(1, chips)]
    for peer in peers:
        pl.semaphore_signal(barrier, inc=1, device_id=peer, device_id_type=MESH)
    pl.semaphore_wait(barrier, len(peers))

    def remote(src, dst, send, recv, dev):
        return pltpu.make_async_remote_copy(
            src_ref=src, dst_ref=dst, send_sem=send, recv_sem=recv,
            device_id=dev, device_id_type=MESH,
        )

    def far(part, t):
        return far_sem.at[part * (chips - 1) + t - 1]

    def gather_start(g, part, near, buf, src, start, count):
        at = pl.ds(start, count)
        for t in range(1, chips):
            remote(src, buf.at[me, at], send_sem.at[g], far(part, t),
                   (h, lax.rem(me + 2 * t, rad))).start()
        remote(src, buf.at[me, at], send_sem.at[g], near_sem.at[near], (h, core)).start()

    def gather_relay(g, part, near, buf, start, count):
        at = pl.ds(start, count)
        for t in range(1, chips):
            k = lax.rem(me + rad - 2 * t, rad)
            remote(buf.at[k, at], buf.at[k, at], send_sem.at[g], far(part, t),
                   (h, core)).wait_recv()
            remote(buf.at[k, at], buf.at[k, at], send_sem.at[g], near_sem.at[near],
                   (h, core)).start()

    def gather_finish(g, near, buf, start, count):
        every = buf.at[pl.ds(0, chips), pl.ds(start, count)]
        remote(every, every, send_sem.at[g], near_sem.at[near], (h, core)).wait_recv()

    def gather_sent(g, buf):
        every = buf.at[pl.ds(0, rad - 1)]
        remote(every, every, send_sem.at[g], near_sem.at[0], (h, core)).wait_send()

    def raw_part(start, count):
        at = pl.ds(start, count)
        return remote(field.at[:, at, pl.ds(0, pair)], don01.at[:, at, :],
                      don_sem.at[0], don_sem.at[1], (across, me))

    head = max(rdev // 8, 16)
    applied = remote(vbuf, don23, don_sem.at[0], don_sem.at[2], (across, me))
    raw_part(0, head).start()
    gather_start(0, 0, 0, gat_u, field.at[:, :, pl.ds(half, pair)], 0, elem)
    load_field.wait()
    row_a, col_a = iota((width, pair), 0), iota((width, pair), 1)

    def pack_rim(above, near_elem, far_elem):
        near = onehot(rim_position(row_a, node, SIDE, above, False) == col_a)
        far = onehot(rim_position(row_a, node, SIDE, above, True) == col_a)
        return (dot(ext[near_elem], near) + dot(ext[far_elem], far)).astype(BF)

    pack[0] = pack_rim(False, HALO + elem - 1, HALO + elem - 2)
    pack[1] = pack_rim(True, HALO, HALO + 1)
    remote(pack.at[0], got.at[0], rim_sem.at[0], rim_sem.at[1], (up, me)).start()
    remote(pack.at[1], got.at[1], rim_sem.at[0], rim_sem.at[1], (down, me)).start()
    raw_part(head, rdev - head).start()
    for cp in load_small:
        cp.wait()
    tile_t = onehot(iota((width, node), 0) % node == iota((width, node), 1))
    tile = onehot(iota((node, width), 1) % node == iota((node, width), 0))
    lrow, lcol = iota((width, width), 0), iota((width, width), 1)
    same = lrow // node == lcol // node

    def spread(block, tt, t, keep):
        return jnp.where(keep, dot(dot(tt, block).astype(BF), t), 0.0).astype(BF)

    both = deriv[...]
    grad_w[:, 0 * width:1 * width] = spread(both[:, :node], tile_t, tile, same)
    grad_w[:, 1 * width:2 * width] = spread(both[:, node:], tile_t, tile, same)
    match = lrow % node == lcol % node
    grad_w[:, 2 * width:3 * width] = onehot(match & (lrow // node == 0))
    grad_w[:, 3 * width:4 * width] = onehot(match & (lrow // node == 1))
    face_t = dot(face[...], tile).astype(BF)
    flane, fcol = iota((width, 4 * SIDE), 0) % node, iota((width, 4 * SIDE), 1)
    fi, fj, fq = flane // SIDE, flane % SIDE, fcol % SIDE
    for s in range(4):
        fixed, free = (fi, fj) if s < 2 else (fj, fi)
        at = SIDE - 1 if s % 2 == 0 else 0
        pick = onehot((fcol // SIDE == s) & (fixed == at) & (free == fq))
        face_w[s] = jnp.where(same, dot(pick, face_t), 0.0).astype(BF)
    ptile_t = onehot(iota((pair, node), 0) % node == iota((pair, node), 1))
    ptile = onehot(iota((node, pair), 1) % node == iota((node, pair), 0))
    psame = iota((pair, pair), 0) // node == iota((pair, pair), 1) // node
    for m in range(nmat):
        blocks[m] = spread(interp[m], ptile_t, ptile, psame)

    gat_u[me] = own[:, :, half:]
    inside = list(range(HALO, elem - HALO))
    listed = inside + [e for e in range(elem) if e not in inside]

    def local_stage(slot):
        e = listed[slot]
        u = ext[HALO + e]
        g = dot(u, grad_w[...])
        flux = g[:, 2 * width:3 * width] * g[:, :width] + g[:, 3 * width:] * g[:, width:2 * width]
        total = -flux
        for s in range(4):
            at = lax.rem(nbr[s, e] - first + HALO + elements, elements)
            at = jnp.minimum(at, elem + 2 * HALO - 1)
            total = total + dot(ext[at], face_w[s])
        gat_s[me, slot] = total[:, half:].astype(BF)
        local01[e] = total[:, :pair] + u[:, :pair].astype(F32)

    cuts = ((0, len(inside)), (len(inside), elem - len(inside)))

    def send_cut(c):
        start, count = cuts[c]
        gather_start(1, 1 + c, 1, gat_s, gat_s.at[me, pl.ds(start, count)], start, count)

    for slot in range(*cuts[0]):
        local_stage(slot)

    lane = iota((rdev, 2 * pair), 1) % pair

    def radial_apply(which, buf, e):
        both_rows = rows[2 * which:2 * which + 2].reshape(2 * rdev, order)
        cols = jnp.concatenate(
            [buf[:, e].reshape(order, pair), buf[:, e + 1].reshape(order, pair)], axis=1
        )
        y = dot(both_rows, cols)
        return jnp.where(lane < node, y[:rdev], y[rdev:])

    gather_relay(0, 0, 0, gat_u, 0, elem)
    send_cut(0)
    gather_finish(0, 0, gat_u, 0, elem)
    load_rows.wait()
    for e in range(0, elem, 2):
        v = radial_apply(1, gat_u, e)
        for k in range(2):
            part = v[:, k * pair:(k + 1) * pair]
            acc23[e + k] = part
            vbuf[e + k] = part.astype(BF)

    remote(pack, got, rim_sem.at[0], rim_sem.at[1], (up, me)).wait_recv()
    row_b, col_b = iota((pair, width), 0), iota((pair, width), 1)

    def unpack(side, above, far):
        place = onehot(rim_position(col_b, node, SIDE, above, far) == row_b)
        return dot(got[side], place).astype(BF)

    ext[0] = unpack(0, False, True)
    ext[1] = unpack(0, False, False)
    ext[HALO + elem] = unpack(1, True, False)
    ext[HALO + elem + 1] = unpack(1, True, True)

    for slot in range(cuts[1][0], elem):
        local_stage(slot)
    send_cut(1)

    def donors(src, e):
        total = None
        for d in range(ndon):
            at = lax.rem(don_id[d, e] - first - elements // 2 + 2 * elements, elements)
            at = jnp.minimum(at, elem - 1)
            term = dot(src[at], blocks[don_mat[d, e]])
            total = term if total is None else total + term
        return total

    remote(don01, don01, don_sem.at[0], don_sem.at[1], (across, me)).wait_recv()

    @pl.when(inner)
    def _():
        applied.start()
    parts = 2
    step = elem // parts
    for c in range(parts):
        for e in range(c * step, (c + 1) * step):
            gat_a[me, e] = (local01[e] + donors(don01, e)).astype(BF)
        gather_start(2, 3 + c, 2 + c, gat_a, gat_a.at[me, pl.ds(c * step, step)], c * step, step)

    for c, (start, count) in enumerate(cuts):
        gather_relay(1, 1 + c, 1, gat_s, start, count)
    gather_finish(1, 1, gat_s, 0, elem)
    for slot in range(0, elem, 2):
        v = radial_apply(1, gat_s, slot)
        for k in range(2):
            acc23[listed[slot + k]] += v[:, k * pair:(k + 1) * pair]

    @pl.when(outer)
    def _():
        applied.start()

    for c in range(parts):
        gather_relay(2, 3 + c, 2 + c, gat_a, c * step, step)
    for c in range(parts):
        gather_finish(2, 2 + c, gat_a, c * step, step)
        for e in range(c * step, (c + 1) * step, 2):
            v = radial_apply(0, gat_a, e).astype(BF)
            for k in range(2):
                out[e + k, :, 0:pair] = v[:, k * pair:(k + 1) * pair]

    applied.wait_recv()
    for e in range(elem):
        out[e, :, half:] = (acc23[e] + donors(don23, e)).astype(BF)

    for g, buf in enumerate((gat_u, gat_s, gat_a)):
        gather_sent(g, buf)
    remote(pack, got, rim_sem.at[0], rim_sem.at[1], (up, me)).wait_send()
    remote(gat_u.at[pl.ds(0, 2)], gat_u.at[pl.ds(0, 2)], don_sem.at[0], don_sem.at[1],
           (across, me)).wait_send()


def on_device(field_state, deriv_pair, face_blocks, interp_blocks, radial_ops,
              neighbours, donor_ids, donor_mats):
    elem, rdev, width = field_state.shape
    node = deriv_pair.shape[0]
    nf = width // node
    horiz, rad = lax.axis_size("horiz"), lax.axis_size("rad")
    nmat, ndon = interp_blocks.shape[0], donor_ids.shape[1]
    order, pair = rad * rdev, 2 * node
    dims = (horiz, rad, elem, rdev, nf, node, nmat, ndon)
    anyspec = pl.BlockSpec(memory_space=pl.ANY)
    vspec = pl.BlockSpec(memory_space=pltpu.VMEM)
    dma = pltpu.SemaphoreType.DMA
    return pl.pallas_call(
        functools.partial(kernel, dims),
        out_shape=pltpu.VMEM(field_state.shape, field_state.dtype),
        in_specs=[anyspec] * 8,
        out_specs=vspec,
        scratch_shapes=[
            pltpu.VMEM((elem + 2 * HALO, rdev, width), BF),
            pltpu.VMEM((nf, rdev, order), BF),
            pltpu.VMEM((2, rdev, pair), BF),
            pltpu.VMEM((2, rdev, pair), BF),
            pltpu.VMEM((width, 4 * width), BF),
            pltpu.VMEM((4, width, width), BF),
            pltpu.VMEM((nmat, pair, pair), BF),
            pltpu.VMEM((rad, elem, rdev, pair), BF),
            pltpu.VMEM((rad, elem, rdev, pair), BF),
            pltpu.VMEM((rad, elem, rdev, pair), BF),
            pltpu.VMEM((elem, rdev, pair), F32),
            pltpu.VMEM((elem, rdev, pair), F32),
            pltpu.VMEM((elem, rdev, pair), BF),
            pltpu.VMEM((elem, rdev, pair), BF),
            pltpu.VMEM((elem, rdev, pair), BF),
            pltpu.SMEM(neighbours.shape[::-1], jnp.int32),
            pltpu.SMEM(donor_ids.shape[::-1], jnp.int32),
            pltpu.SMEM(donor_mats.shape[::-1], jnp.int32),
            pltpu.VMEM(deriv_pair.shape, BF),
            pltpu.VMEM(face_blocks.shape, BF),
            pltpu.VMEM(interp_blocks.shape, BF),
            dma((8,)),
            dma((2,)),
            dma((3,)),
            dma((3,)),
            dma((5 * (rad // 2 - 1),)),
            dma((4,)),
            pltpu.SemaphoreType.REGULAR,
        ],
        compiler_params=pltpu.CompilerParams(collective_id=0, has_side_effects=True, vmem_limit_bytes=57000 * 1024),
    )(field_state, deriv_pair, face_blocks, interp_blocks, radial_ops,
      neighbours.T, donor_ids.T, donor_mats.T)


def solution(mesh):
    in_specs = (
        P("horiz", "rad", None), P(), P(), P(), P(),
        P("horiz", None), P("horiz", None), P("horiz", None),
    )
    return jax.shard_map(
        on_device, mesh=mesh, in_specs=in_specs, out_specs=P("horiz", "rad", None),
        check_vma=False,
    )
```

```python
import functools

import jax
import jax.numpy as jnp
from jax import lax
from jax.experimental import pallas as pl
from jax.experimental.pallas import tpu as pltpu
from jax.sharding import PartitionSpec as P

SIDE = 8
HALO = 2
MESH = pl.DeviceIdType.MESH
BF = jnp.bfloat16
F32 = jnp.float32


def dot(a, b):
    return jnp.dot(a, b, preferred_element_type=F32)


def iota(shape, dim):
    return lax.broadcasted_iota(jnp.int32, shape, dim)


def onehot(mask):
    return jnp.where(mask, 1.0, 0.0).astype(BF)


def rim_position(lane, node, side, above, far):
    field, n = lane // node, lane % node
    i, j = n // side, n % side
    last = 0 if above else side - 1
    base = field * (node // 2)
    if far:
        return jnp.where(j == last, base + 2 * side + i, -1)
    return jnp.where(i == last, base + j, jnp.where(j == last, base + side + i, -1))


def kernel(
    dims,
    field, deriv_in, face_in, interp_in, radial, nbr_in, don_id_in, don_mat_in,
    out,
    ext, rows, pack, got, grad_w, face_w, blocks,
    gat_u, gat_s, gat_a, local01, acc23, vbuf, don01, don23,
    nbr, don_id, don_mat, deriv, face, interp,
    local_sem, rim_sem, don_sem, send_sem, far_sem, near_sem, ready,
):
    horiz, rad, elem, rdev, nf, node, nmat, ndon = dims
    width = nf * node
    pair = 2 * node
    half = width - pair
    order = rad * rdev
    chips = rad // 2
    h, me = lax.axis_index("horiz"), lax.axis_index("rad")
    elements = elem * horiz
    first = h * elem
    up, down = lax.rem(h + 1, horiz), lax.rem(h + horiz - 1, horiz)
    across = lax.rem(h + horiz // 2, horiz)
    second = lax.rem(me, 2)
    core = me + 1 - 2 * second
    base = me - second
    quarter = horiz // 4
    outer = h >= horiz - quarter
    inner = jnp.logical_not(outer)
    own = ext.at[pl.ds(HALO, elem)]

    load_field = pltpu.make_async_copy(field, own, local_sem.at[0])
    load_rows = pltpu.make_async_copy(
        radial.at[:, pl.ds(pl.multiple_of(me * rdev, rdev), rdev), :], rows, local_sem.at[1]
    )
    load_field.start()
    load_small = [pltpu.make_async_copy(a, b, local_sem.at[2 + i]) for i, (a, b) in enumerate(
        ((deriv_in, deriv), (face_in, face), (interp_in, interp),
         (nbr_in, nbr), (don_id_in, don_id), (don_mat_in, don_mat)))]
    for cp in load_small:
        cp.start()
    load_rows.start()

    barrier = pltpu.get_barrier_semaphore()
    peers = [(up, me), (down, me), (across, me), (h, core)]
    peers += [(h, lax.rem(me + 2 * t, rad)) for t in range(1, chips)]
    for peer in peers:
        pl.semaphore_signal(barrier, inc=1, device_id=peer, device_id_type=MESH)
    pl.semaphore_wait(barrier, len(peers))

    def remote(src, dst, send, recv, dev):
        return pltpu.make_async_remote_copy(
            src_ref=src, dst_ref=dst, send_sem=send, recv_sem=recv,
            device_id=dev, device_id_type=MESH,
        )

    def far(part, t):
        return far_sem.at[part * (chips - 1) + t - 1]

    def gather_start(g, part, near, buf, src, start, count):
        at = pl.ds(start, count)
        for t in range(1, chips):
            remote(src, buf.at[me, at], send_sem.at[g], far(part, t),
                   (h, lax.rem(me + 2 * t, rad))).start()
        remote(src, buf.at[me, at], send_sem.at[g], near_sem.at[near], (h, core)).start()

    def gather_relay(g, part, near, buf, start, count):
        at = pl.ds(start, count)
        for t in range(1, chips):
            k = lax.rem(me + rad - 2 * t, rad)
            remote(buf.at[k, at], buf.at[k, at], send_sem.at[g], far(part, t),
                   (h, core)).wait_recv()
            remote(buf.at[k, at], buf.at[k, at], send_sem.at[g], near_sem.at[near],
                   (h, core)).start()

    def gather_finish(g, near, buf, start, count):
        every = buf.at[pl.ds(0, chips), pl.ds(start, count)]
        remote(every, every, send_sem.at[g], near_sem.at[near], (h, core)).wait_recv()

    def gather_sent(g, buf):
        every = buf.at[pl.ds(0, rad - 1)]
        remote(every, every, send_sem.at[g], near_sem.at[0], (h, core)).wait_send()

    def raw_part(start, count):
        at = pl.ds(start, count)
        return remote(own.at[:, at, pl.ds(0, pair)], don01.at[:, at, :],
                      don_sem.at[0], don_sem.at[1], (across, me))

    head = max(rdev // 8, 16)
    applied = remote(vbuf, don23, don_sem.at[0], don_sem.at[2], (across, me))
    gather_start(0, 0, 0, gat_u, field.at[:, :, pl.ds(half, pair)], 0, elem)
    load_field.wait()
    raw_part(0, head).start()
    row_a, col_a = iota((width, pair), 0), iota((width, pair), 1)

    def pack_rim(above, near_elem, far_elem):
        near = onehot(rim_position(row_a, node, SIDE, above, False) == col_a)
        far = onehot(rim_position(row_a, node, SIDE, above, True) == col_a)
        return (dot(ext[near_elem], near) + dot(ext[far_elem], far)).astype(BF)

    pack[0] = pack_rim(False, HALO + elem - 1, HALO + elem - 2)
    pack[1] = pack_rim(True, HALO, HALO + 1)
    remote(pack.at[0], got.at[0], rim_sem.at[0], rim_sem.at[1], (up, me)).start()
    remote(pack.at[1], got.at[1], rim_sem.at[0], rim_sem.at[1], (down, me)).start()
    raw_part(head, rdev - head).start()
    for cp in load_small:
        cp.wait()
    tile_t = onehot(iota((width, node), 0) % node == iota((width, node), 1))
    tile = onehot(iota((node, width), 1) % node == iota((node, width), 0))
    lrow, lcol = iota((width, width), 0), iota((width, width), 1)
    same = lrow // node == lcol // node

    def spread(block, tt, t, keep):
        return jnp.where(keep, dot(dot(tt, block).astype(BF), t), 0.0).astype(BF)

    both = deriv[...]
    grad_w[:, 0 * width:1 * width] = spread(both[:, :node], tile_t, tile, same)
    grad_w[:, 1 * width:2 * width] = spread(both[:, node:], tile_t, tile, same)
    match = lrow % node == lcol % node
    grad_w[:, 2 * width:3 * width] = onehot(match & (lrow // node == 0))
    grad_w[:, 3 * width:4 * width] = onehot(match & (lrow // node == 1))
    face_t = dot(face[...], tile).astype(BF)
    flane, fcol = iota((width, 4 * SIDE), 0) % node, iota((width, 4 * SIDE), 1)
    fi, fj, fq = flane // SIDE, flane % SIDE, fcol % SIDE
    for s in range(4):
        fixed, free = (fi, fj) if s < 2 else (fj, fi)
        at = SIDE - 1 if s % 2 == 0 else 0
        pick = onehot((fcol // SIDE == s) & (fixed == at) & (free == fq))
        face_w[s] = jnp.where(same, dot(pick, face_t), 0.0).astype(BF)
    ptile_t = onehot(iota((pair, node), 0) % node == iota((pair, node), 1))
    ptile = onehot(iota((node, pair), 1) % node == iota((node, pair), 0))
    psame = iota((pair, pair), 0) // node == iota((pair, pair), 1) // node
    for m in range(nmat):
        blocks[m] = spread(interp[m], ptile_t, ptile, psame)

    gat_u[me] = own[:, :, half:]
    inside = list(range(HALO, elem - HALO))
    listed = inside + [e for e in range(elem) if e not in inside]

    def local_stage(slot):
        e = listed[slot]
        u = ext[HALO + e]
        g = dot(u, grad_w[...])
        flux = g[:, 2 * width:3 * width] * g[:, :width] + g[:, 3 * width:] * g[:, width:2 * width]
        total = -flux
        for s in range(4):
            at = lax.rem(nbr[s, e] - first + HALO + elements, elements)
            at = jnp.minimum(at, elem + 2 * HALO - 1)
            total = total + dot(ext[at], face_w[s])
        gat_s[me, slot] = total[:, half:].astype(BF)
        local01[e] = total[:, :pair] + u[:, :pair].astype(F32)

    cuts = ((0, len(inside)), (len(inside), elem - len(inside)))

    def send_cut(c):
        start, count = cuts[c]
        gather_start(1, 1 + c, 1, gat_s, gat_s.at[me, pl.ds(start, count)], start, count)

    for slot in range(*cuts[0]):
        local_stage(slot)

    lane = iota((rdev, 2 * pair), 1) % pair

    def radial_apply(which, buf, e):
        both_rows = rows[2 * which:2 * which + 2].reshape(2 * rdev, order)
        cols = jnp.concatenate(
            [buf[:, e].reshape(order, pair), buf[:, e + 1].reshape(order, pair)], axis=1
        )
        y = dot(both_rows, cols)
        return jnp.where(lane < node, y[:rdev], y[rdev:])

    gather_relay(0, 0, 0, gat_u, 0, elem)
    send_cut(0)
    gather_finish(0, 0, gat_u, 0, elem)
    load_rows.wait()
    for e in range(0, elem, 2):
        v = radial_apply(1, gat_u, e)
        for k in range(2):
            part = v[:, k * pair:(k + 1) * pair]
            acc23[e + k] = part
            vbuf[e + k] = part.astype(BF)

    remote(pack, got, rim_sem.at[0], rim_sem.at[1], (up, me)).wait_recv()
    row_b, col_b = iota((pair, width), 0), iota((pair, width), 1)

    def unpack(side, above, far):
        place = onehot(rim_position(col_b, node, SIDE, above, far) == row_b)
        return dot(got[side], place).astype(BF)

    ext[0] = unpack(0, False, True)
    ext[1] = unpack(0, False, False)
    ext[HALO + elem] = unpack(1, True, False)
    ext[HALO + elem + 1] = unpack(1, True, True)

    for slot in range(cuts[1][0], elem):
        local_stage(slot)
    send_cut(1)

    def donors(src, e):
        total = None
        for d in range(ndon):
            at = lax.rem(don_id[d, e] - first - elements // 2 + 2 * elements, elements)
            at = jnp.minimum(at, elem - 1)
            term = dot(src[at], blocks[don_mat[d, e]])
            total = term if total is None else total + term
        return total

    remote(don01, don01, don_sem.at[0], don_sem.at[1], (across, me)).wait_recv()

    @pl.when(inner)
    def _():
        applied.start()

    parts = 1
    step = elem // parts
    for c in range(parts):
        for e in range(c * step, (c + 1) * step):
            gat_a[me, e] = (local01[e] + donors(don01, e)).astype(BF)
        gather_start(2, 3 + c, 2 + c, gat_a, gat_a.at[me, pl.ds(c * step, step)], c * step, step)

    for c, (start, count) in enumerate(cuts):
        gather_relay(1, 1 + c, 1, gat_s, start, count)
    gather_finish(1, 1, gat_s, 0, elem)
    for slot in range(0, elem, 2):
        v = radial_apply(1, gat_s, slot)
        for k in range(2):
            acc23[listed[slot + k]] += v[:, k * pair:(k + 1) * pair]


    @pl.when(outer)
    def _():
        applied.start()

    for c in range(parts):
        gather_relay(2, 3 + c, 2 + c, gat_a, c * step, step)
    for c in range(parts):
        gather_finish(2, 2 + c, gat_a, c * step, step)
        for e in range(c * step, (c + 1) * step, 2):
            v = radial_apply(0, gat_a, e).astype(BF)
            for k in range(2):
                out[e + k, :, 0:pair] = v[:, k * pair:(k + 1) * pair]

    applied.wait_recv()
    for e in range(elem):
        out[e, :, half:] = (acc23[e] + donors(don23, e)).astype(BF)

    for g, buf in enumerate((gat_u, gat_s, gat_a)):
        gather_sent(g, buf)
    remote(pack, got, rim_sem.at[0], rim_sem.at[1], (up, me)).wait_send()
    twice = gat_u.at[pl.ds(0, 2)]
    remote(twice, twice, don_sem.at[0], don_sem.at[1], (across, me)).wait_send()


def on_device(field_state, deriv_pair, face_blocks, interp_blocks, radial_ops,
              neighbours, donor_ids, donor_mats):
    elem, rdev, width = field_state.shape
    node = deriv_pair.shape[0]
    nf = width // node
    horiz, rad = lax.axis_size("horiz"), lax.axis_size("rad")
    nmat, ndon = interp_blocks.shape[0], donor_ids.shape[1]
    order, pair = rad * rdev, 2 * node
    dims = (horiz, rad, elem, rdev, nf, node, nmat, ndon)
    anyspec = pl.BlockSpec(memory_space=pl.ANY)
    vspec = pl.BlockSpec(memory_space=pltpu.VMEM)
    dma = pltpu.SemaphoreType.DMA
    return pl.pallas_call(
        functools.partial(kernel, dims),
        out_shape=pltpu.VMEM(field_state.shape, field_state.dtype),
        in_specs=[anyspec] * 8,
        out_specs=vspec,
        scratch_shapes=[
            pltpu.VMEM((elem + 2 * HALO, rdev, width), BF),
            pltpu.VMEM((nf, rdev, order), BF),
            pltpu.VMEM((2, rdev, pair), BF),
            pltpu.VMEM((2, rdev, pair), BF),
            pltpu.VMEM((width, 4 * width), BF),
            pltpu.VMEM((4, width, width), BF),
            pltpu.VMEM((nmat, pair, pair), BF),
            pltpu.VMEM((rad, elem, rdev, pair), BF),
            pltpu.VMEM((rad, elem, rdev, pair), BF),
            pltpu.VMEM((rad, elem, rdev, pair), BF),
            pltpu.VMEM((elem, rdev, pair), F32),
            pltpu.VMEM((elem, rdev, pair), F32),
            pltpu.VMEM((elem, rdev, pair), BF),
            pltpu.VMEM((elem, rdev, pair), BF),
            pltpu.VMEM((elem, rdev, pair), BF),
            pltpu.SMEM(neighbours.shape[::-1], jnp.int32),
            pltpu.SMEM(donor_ids.shape[::-1], jnp.int32),
            pltpu.SMEM(donor_mats.shape[::-1], jnp.int32),
            pltpu.VMEM(deriv_pair.shape, BF),
            pltpu.VMEM(face_blocks.shape, BF),
            pltpu.VMEM(interp_blocks.shape, BF),
            dma((8,)),
            dma((2,)),
            dma((3,)),
            dma((3,)),
            dma((4 * (rad // 2 - 1),)),
            dma((3,)),
            pltpu.SemaphoreType.REGULAR,
        ],
        compiler_params=pltpu.CompilerParams(collective_id=0, has_side_effects=True, vmem_limit_bytes=57000 * 1024),
    )(field_state, deriv_pair, face_blocks, interp_blocks, radial_ops,
      neighbours.T, donor_ids.T, donor_mats.T)


def solution(mesh):
    in_specs = (
        P("horiz", "rad", None), P(), P(), P(), P(),
        P("horiz", None), P("horiz", None), P("horiz", None),
    )
    return jax.shard_map(
        on_device, mesh=mesh, in_specs=in_specs, out_specs=P("horiz", "rad", None),
        check_vma=False,
    )
```

```python
import functools

import jax
import jax.numpy as jnp
from jax import lax
from jax.experimental import pallas as pl
from jax.experimental.pallas import tpu as pltpu
from jax.sharding import PartitionSpec as P

SIDE = 8
HALO = 2
MESH = pl.DeviceIdType.MESH
BF = jnp.bfloat16
F32 = jnp.float32


def dot(a, b):
    return jnp.dot(a, b, preferred_element_type=F32)


def iota(shape, dim):
    return lax.broadcasted_iota(jnp.int32, shape, dim)


def onehot(mask):
    return jnp.where(mask, 1.0, 0.0).astype(BF)


def rim_position(lane, node, side, above, far):
    field, n = lane // node, lane % node
    i, j = n // side, n % side
    last = 0 if above else side - 1
    base = field * (3 * side)
    if far:
        return jnp.where(j == last, base + 2 * side + i, -1)
    return jnp.where(i == last, base + j, jnp.where(j == last, base + side + i, -1))


def kernel(
    dims,
    field, deriv_in, face_in, interp_in, radial, nbr_in, don_id_in, don_mat_in,
    out,
    ext, rows, pack, got, grad_w, face_w, blocks,
    gat_u, gat_s, gat_a, local01, acc23, vbuf, don01, don23,
    nbr, don_id, don_mat, deriv, face, interp,
    local_sem, rim_sem, don_sem, send_sem, far_sem, near_sem, ready,
):
    horiz, rad, elem, rdev, nf, node, nmat, ndon = dims
    width = nf * node
    pair = 2 * node
    half = width - pair
    order = rad * rdev
    chips = rad // 2
    h, me = lax.axis_index("horiz"), lax.axis_index("rad")
    elements = elem * horiz
    first = h * elem
    up, down = lax.rem(h + 1, horiz), lax.rem(h + horiz - 1, horiz)
    across = lax.rem(h + horiz // 2, horiz)
    second = lax.rem(me, 2)
    core = me + 1 - 2 * second
    base = me - second
    quarter = horiz // 4
    outer = h >= horiz - quarter
    inner = jnp.logical_not(outer)
    own = ext.at[pl.ds(HALO, elem)]

    load_field = pltpu.make_async_copy(field, own, local_sem.at[0])
    load_rows = pltpu.make_async_copy(
        radial.at[:, pl.ds(pl.multiple_of(me * rdev, rdev), rdev), :], rows, local_sem.at[1]
    )
    load_field.start()
    load_small = [pltpu.make_async_copy(a, b, local_sem.at[2 + i]) for i, (a, b) in enumerate(
        ((deriv_in, deriv), (face_in, face), (interp_in, interp),
         (nbr_in, nbr), (don_id_in, don_id), (don_mat_in, don_mat)))]
    for cp in load_small:
        cp.start()
    load_rows.start()

    barrier = pltpu.get_barrier_semaphore()
    peers = [
        (across, jnp.where(across == 0, base, me)),
        (up, jnp.where(up == 0, base + 1, me)),
        (down, jnp.where(down == 0, base, me)),
        (h, core),
    ]
    peers += [(h, lax.rem(jnp.where(h == 0, base, me) + 2 * t, rad)) for t in range(1, chips)]
    for peer in peers:
        pl.semaphore_signal(barrier, inc=1, device_id=peer, device_id_type=MESH)

    @pl.when(h != 0)
    def _():
        pl.semaphore_wait(barrier, len(peers))

    @pl.when((h == 0) & (second == 0))
    def _():
        pl.semaphore_wait(barrier, 2 * chips + 3)
        pl.semaphore_signal(ready, inc=1, device_id=(h, core), device_id_type=MESH)

    @pl.when((h == 0) & (second == 1))
    def _():
        pl.semaphore_wait(ready, 1)

    def remote(src, dst, send, recv, dev):
        return pltpu.make_async_remote_copy(
            src_ref=src, dst_ref=dst, send_sem=send, recv_sem=recv,
            device_id=dev, device_id_type=MESH,
        )

    def far(part, t):
        return far_sem.at[part * (chips - 1) + t - 1]

    def gather_start(g, part, near, buf, src, start, count):
        at = pl.ds(start, count)
        for t in range(1, chips):
            remote(src, buf.at[me, at], send_sem.at[g], far(part, t),
                   (h, lax.rem(me + 2 * t, rad))).start()
        remote(src, buf.at[me, at], send_sem.at[g], near_sem.at[near], (h, core)).start()

    def gather_relay(g, part, near, buf, start, count):
        at = pl.ds(start, count)
        for t in range(1, chips):
            k = lax.rem(me + rad - 2 * t, rad)
            remote(buf.at[k, at], buf.at[k, at], send_sem.at[g], far(part, t),
                   (h, core)).wait_recv()
            remote(buf.at[k, at], buf.at[k, at], send_sem.at[g], near_sem.at[near],
                   (h, core)).start()

    def gather_finish(g, near, buf, start, count):
        every = buf.at[pl.ds(0, chips), pl.ds(start, count)]
        remote(every, every, send_sem.at[g], near_sem.at[near], (h, core)).wait_recv()

    def gather_sent(g, buf):
        every = buf.at[pl.ds(0, rad - 1)]
        remote(every, every, send_sem.at[g], near_sem.at[0], (h, core)).wait_send()

    def raw_part(start, count):
        at = pl.ds(start, count)
        return remote(own.at[:, at, pl.ds(0, pair)], don01.at[:, at, :],
                      don_sem.at[0], don_sem.at[1], (across, me))

    head = max(rdev // 8, 16)
    applied = remote(vbuf, don23, don_sem.at[0], don_sem.at[2], (across, me))
    gather_start(0, 0, 0, gat_u, field.at[:, :, pl.ds(half, pair)], 0, elem)
    load_field.wait()
    raw_part(0, head).start()
    rim = nf * 3 * SIDE
    row_a, col_a = iota((rim, width), 0), iota((rim, width), 1)

    def across_lanes(place, u):
        return lax.dot_general(place, u, (((1,), (1,)), ((), ())), preferred_element_type=F32)

    def pack_rim(above, near_elem, far_elem):
        near = onehot(rim_position(col_a, node, SIDE, above, False) == row_a)
        far = onehot(rim_position(col_a, node, SIDE, above, True) == row_a)
        return (across_lanes(near, ext[near_elem]) + across_lanes(far, ext[far_elem])).astype(BF)

    pack[0] = pack_rim(False, HALO + elem - 1, HALO + elem - 2)
    pack[1] = pack_rim(True, HALO, HALO + 1)
    remote(pack.at[0], got.at[0], rim_sem.at[0], rim_sem.at[1], (up, me)).start()
    rim_down = remote(pack.at[1], got.at[1], rim_sem.at[0], rim_sem.at[1], (down, me))

    @pl.when(h != 0)
    def _():
        rim_down.start()

    raw_part(head, rdev - head).start()
    for cp in load_small:
        cp.wait()
    tile_t = onehot(iota((width, node), 0) % node == iota((width, node), 1))
    tile = onehot(iota((node, width), 1) % node == iota((node, width), 0))
    lrow, lcol = iota((width, width), 0), iota((width, width), 1)
    same = lrow // node == lcol // node

    def spread(block, tt, t, keep):
        return jnp.where(keep, dot(dot(tt, block).astype(BF), t), 0.0).astype(BF)

    both = deriv[...]
    grad_w[:, 0 * width:1 * width] = spread(both[:, :node], tile_t, tile, same)
    grad_w[:, 1 * width:2 * width] = spread(both[:, node:], tile_t, tile, same)
    match = lrow % node == lcol % node
    grad_w[:, 2 * width:3 * width] = onehot(match & (lrow // node == 0))
    grad_w[:, 3 * width:4 * width] = onehot(match & (lrow // node == 1))
    face_t = dot(face[...], tile).astype(BF)
    flane, fcol = iota((width, 4 * SIDE), 0) % node, iota((width, 4 * SIDE), 1)
    fi, fj, fq = flane // SIDE, flane % SIDE, fcol % SIDE
    for s in range(4):
        fixed, free = (fi, fj) if s < 2 else (fj, fi)
        at = SIDE - 1 if s % 2 == 0 else 0
        pick = onehot((fcol // SIDE == s) & (fixed == at) & (free == fq))
        face_w[s] = jnp.where(same, dot(pick, face_t), 0.0).astype(BF)
    ptile_t = onehot(iota((pair, node), 0) % node == iota((pair, node), 1))
    ptile = onehot(iota((node, pair), 1) % node == iota((node, pair), 0))
    psame = iota((pair, pair), 0) // node == iota((pair, pair), 1) // node
    for m in range(nmat):
        blocks[m] = spread(interp[m], ptile_t, ptile, psame)

    @pl.when((h == 0) & (second == 1))
    def _():
        pl.semaphore_wait(barrier, 3)
        pl.semaphore_signal(ready, inc=1, device_id=(h, core), device_id_type=MESH)

    @pl.when((h == 0) & (second == 0))
    def _():
        pl.semaphore_wait(ready, 1)

    @pl.when(h == 0)
    def _():
        rim_down.start()

    gat_u[me] = own[:, :, half:]
    inside = list(range(HALO, elem - HALO))
    listed = inside + [e for e in range(elem) if e not in inside]

    def local_stage(slot):
        e = listed[slot]
        u = ext[HALO + e]
        g = dot(u, grad_w[...])
        flux = g[:, 2 * width:3 * width] * g[:, :width] + g[:, 3 * width:] * g[:, width:2 * width]
        total = -flux
        for s in range(4):
            at = lax.rem(nbr[s, e] - first + HALO + elements, elements)
            at = jnp.minimum(at, elem + 2 * HALO - 1)
            total = total + dot(ext[at], face_w[s])
        gat_s[me, slot] = total[:, half:].astype(BF)
        local01[e] = total[:, :pair] + u[:, :pair].astype(F32)

    cuts = ((0, len(inside)), (len(inside), elem - len(inside)))

    def send_cut(c):
        start, count = cuts[c]
        gather_start(1, 1 + c, 1, gat_s, gat_s.at[me, pl.ds(start, count)], start, count)

    for slot in range(*cuts[0]):
        local_stage(slot)

    lane = iota((rdev, 2 * pair), 1) % pair

    def radial_apply(which, buf, e):
        both_rows = rows[2 * which:2 * which + 2].reshape(2 * rdev, order)
        cols = jnp.concatenate(
            [buf[:, e].reshape(order, pair), buf[:, e + 1].reshape(order, pair)], axis=1
        )
        y = dot(both_rows, cols)
        return jnp.where(lane < node, y[:rdev], y[rdev:])

    gather_relay(0, 0, 0, gat_u, 0, elem)
    send_cut(0)
    gather_finish(0, 0, gat_u, 0, elem)
    load_rows.wait()
    for e in range(0, elem, 2):
        v = radial_apply(1, gat_u, e)
        for k in range(2):
            part = v[:, k * pair:(k + 1) * pair]
            acc23[e + k] = part
            vbuf[e + k] = part.astype(BF)

    remote(pack, got, rim_sem.at[0], rim_sem.at[1], (up, me)).wait_recv()

    def unpack(side, above, far):
        place = onehot(rim_position(col_a, node, SIDE, above, far) == row_a)
        return lax.dot_general(got[side], place, (((0,), (0,)), ((), ())),
                               preferred_element_type=F32).astype(BF)

    ext[0] = unpack(0, False, True)
    ext[1] = unpack(0, False, False)
    ext[HALO + elem] = unpack(1, True, False)
    ext[HALO + elem + 1] = unpack(1, True, True)

    for slot in range(cuts[1][0], elem):
        local_stage(slot)
    send_cut(1)

    def donors(src, e):
        total = None
        for d in range(ndon):
            at = lax.rem(don_id[d, e] - first - elements // 2 + 2 * elements, elements)
            at = jnp.minimum(at, elem - 1)
            term = dot(src[at], blocks[don_mat[d, e]])
            total = term if total is None else total + term
        return total

    remote(don01, don01, don_sem.at[0], don_sem.at[1], (across, me)).wait_recv()

    @pl.when(inner)
    def _():
        applied.start()

    parts = 1
    step = elem // parts
    for c in range(parts):
        for e in range(c * step, (c + 1) * step):
            gat_a[me, e] = (local01[e] + donors(don01, e)).astype(BF)
        gather_start(2, 3 + c, 2 + c, gat_a, gat_a.at[me, pl.ds(c * step, step)], c * step, step)

    for c, (start, count) in enumerate(cuts):
        gather_relay(1, 1 + c, 1, gat_s, start, count)
    gather_finish(1, 1, gat_s, 0, elem)
    for slot in range(0, elem, 2):
        v = radial_apply(1, gat_s, slot)
        for k in range(2):
            acc23[listed[slot + k]] += v[:, k * pair:(k + 1) * pair]


    @pl.when(outer)
    def _():
        applied.start()

    for c in range(parts):
        gather_relay(2, 3 + c, 2 + c, gat_a, c * step, step)
    for c in range(parts):
        gather_finish(2, 2 + c, gat_a, c * step, step)
        for e in range(c * step, (c + 1) * step, 2):
            v = radial_apply(0, gat_a, e).astype(BF)
            for k in range(2):
                out[e + k, :, 0:pair] = v[:, k * pair:(k + 1) * pair]

    applied.wait_recv()
    for e in range(elem):
        out[e, :, half:] = (acc23[e] + donors(don23, e)).astype(BF)

    for g, buf in enumerate((gat_u, gat_s, gat_a)):
        gather_sent(g, buf)
    remote(pack, got, rim_sem.at[0], rim_sem.at[1], (up, me)).wait_send()
    twice = gat_u.at[pl.ds(0, 2)]
    remote(twice, twice, don_sem.at[0], don_sem.at[1], (across, me)).wait_send()


def on_device(field_state, deriv_pair, face_blocks, interp_blocks, radial_ops,
              neighbours, donor_ids, donor_mats):
    elem, rdev, width = field_state.shape
    node = deriv_pair.shape[0]
    nf = width // node
    horiz, rad = lax.axis_size("horiz"), lax.axis_size("rad")
    nmat, ndon = interp_blocks.shape[0], donor_ids.shape[1]
    order, pair = rad * rdev, 2 * node
    dims = (horiz, rad, elem, rdev, nf, node, nmat, ndon)
    anyspec = pl.BlockSpec(memory_space=pl.ANY)
    vspec = pl.BlockSpec(memory_space=pltpu.VMEM)
    dma = pltpu.SemaphoreType.DMA
    return pl.pallas_call(
        functools.partial(kernel, dims),
        out_shape=pltpu.VMEM(field_state.shape, field_state.dtype),
        in_specs=[anyspec] * 8,
        out_specs=vspec,
        scratch_shapes=[
            pltpu.VMEM((elem + 2 * HALO, rdev, width), BF),
            pltpu.VMEM((nf, rdev, order), BF),
            pltpu.VMEM((2, nf * 3 * SIDE, rdev), BF),
            pltpu.VMEM((2, nf * 3 * SIDE, rdev), BF),
            pltpu.VMEM((width, 4 * width), BF),
            pltpu.VMEM((4, width, width), BF),
            pltpu.VMEM((nmat, pair, pair), BF),
            pltpu.VMEM((rad, elem, rdev, pair), BF),
            pltpu.VMEM((rad, elem, rdev, pair), BF),
            pltpu.VMEM((rad, elem, rdev, pair), BF),
            pltpu.VMEM((elem, rdev, pair), F32),
            pltpu.VMEM((elem, rdev, pair), F32),
            pltpu.VMEM((elem, rdev, pair), BF),
            pltpu.VMEM((elem, rdev, pair), BF),
            pltpu.VMEM((elem, rdev, pair), BF),
            pltpu.SMEM(neighbours.shape[::-1], jnp.int32),
            pltpu.SMEM(donor_ids.shape[::-1], jnp.int32),
            pltpu.SMEM(donor_mats.shape[::-1], jnp.int32),
            pltpu.VMEM(deriv_pair.shape, BF),
            pltpu.VMEM(face_blocks.shape, BF),
            pltpu.VMEM(interp_blocks.shape, BF),
            dma((8,)),
            dma((2,)),
            dma((3,)),
            dma((3,)),
            dma((4 * (rad // 2 - 1),)),
            dma((3,)),
            pltpu.SemaphoreType.REGULAR,
        ],
        compiler_params=pltpu.CompilerParams(collective_id=0, has_side_effects=True, vmem_limit_bytes=57000 * 1024),
    )(field_state, deriv_pair, face_blocks, interp_blocks, radial_ops,
      neighbours.T, donor_ids.T, donor_mats.T)


def solution(mesh):
    in_specs = (
        P("horiz", "rad", None), P(), P(), P(), P(),
        P("horiz", None), P("horiz", None), P("horiz", None),
    )
    return jax.shard_map(
        on_device, mesh=mesh, in_specs=in_specs, out_specs=P("horiz", "rad", None),
        check_vma=False,
    )
```

```python
import functools

import jax
import jax.numpy as jnp
from jax import lax
from jax.experimental import pallas as pl
from jax.experimental.pallas import tpu as pltpu
from jax.sharding import PartitionSpec as P

SIDE = 8
HALO = 2
MESH = pl.DeviceIdType.MESH
BF = jnp.bfloat16
F32 = jnp.float32


def dot(a, b):
    return jnp.dot(a, b, preferred_element_type=F32)


def iota(shape, dim):
    return lax.broadcasted_iota(jnp.int32, shape, dim)


def onehot(mask):
    return jnp.where(mask, 1.0, 0.0).astype(BF)


def rim_position(lane, node, side, above, far):
    field, n = lane // node, lane % node
    i, j = n // side, n % side
    last = 0 if above else side - 1
    base = field * (3 * side)
    if far:
        return jnp.where(j == last, base + 2 * side + i, -1)
    return jnp.where(i == last, base + j, jnp.where(j == last, base + side + i, -1))


def kernel(
    dims,
    field, deriv_in, face_in, interp_in, radial, nbr_in, don_id_in, don_mat_in,
    out,
    ext, rows, pack, got, grad_w, face_w, blocks,
    gat_u, gat_s, gat_a, local01, acc23, vbuf, don01, don23,
    nbr, don_id, don_mat, deriv, face, interp,
    local_sem, rim_sem, don_sem, send_sem, far_sem, near_sem, ready,
):
    horiz, rad, elem, rdev, nf, node, nmat, ndon = dims
    width = nf * node
    pair = 2 * node
    half = width - pair
    order = rad * rdev
    chips = rad // 2
    h, me = lax.axis_index("horiz"), lax.axis_index("rad")
    elements = elem * horiz
    first = h * elem
    up, down = lax.rem(h + 1, horiz), lax.rem(h + horiz - 1, horiz)
    across = lax.rem(h + horiz // 2, horiz)
    second = lax.rem(me, 2)
    core = me + 1 - 2 * second
    base = me - second
    quarter = horiz // 4
    outer = h >= horiz - quarter
    inner = jnp.logical_not(outer)
    last = ((h >= quarter) & (h < 2 * quarter)) | outer
    own = ext.at[pl.ds(HALO, elem)]

    load_field = pltpu.make_async_copy(field, own, local_sem.at[0])
    load_rows = pltpu.make_async_copy(
        radial.at[:, pl.ds(pl.multiple_of(me * rdev, rdev), rdev), :], rows, local_sem.at[1]
    )
    load_field.start()
    load_small = [pltpu.make_async_copy(a, b, local_sem.at[2 + i]) for i, (a, b) in enumerate(
        ((deriv_in, deriv), (face_in, face), (interp_in, interp),
         (nbr_in, nbr), (don_id_in, don_id), (don_mat_in, don_mat)))]
    for cp in load_small:
        cp.start()
    load_rows.start()

    barrier = pltpu.get_barrier_semaphore()
    peers = [
        (across, jnp.where(across == 0, base, me)),
        (up, jnp.where(up == 0, base + 1, me)),
        (down, jnp.where(down == 0, base, me)),
        (h, core),
    ]
    peers += [(h, lax.rem(jnp.where(h == 0, base, me) + 2 * t, rad)) for t in range(1, chips)]
    for peer in peers:
        pl.semaphore_signal(barrier, inc=1, device_id=peer, device_id_type=MESH)

    @pl.when(h != 0)
    def _():
        pl.semaphore_wait(barrier, len(peers))

    @pl.when((h == 0) & (second == 0))
    def _():
        pl.semaphore_wait(barrier, 2 * chips + 3)
        pl.semaphore_signal(ready, inc=1, device_id=(h, core), device_id_type=MESH)

    @pl.when((h == 0) & (second == 1))
    def _():
        pl.semaphore_wait(ready, 1)

    def remote(src, dst, send, recv, dev):
        return pltpu.make_async_remote_copy(
            src_ref=src, dst_ref=dst, send_sem=send, recv_sem=recv,
            device_id=dev, device_id_type=MESH,
        )

    def far(part, t):
        return far_sem.at[part * (chips - 1) + t - 1]

    def gather_start(g, part, near, buf, src, start, count):
        at = pl.ds(start, count)
        for t in range(1, chips):
            remote(src, buf.at[me, at], send_sem.at[g], far(part, t),
                   (h, lax.rem(me + 2 * t, rad))).start()
        remote(src, buf.at[me, at], send_sem.at[g], near_sem.at[near], (h, core)).start()

    def gather_relay(g, part, near, buf, start, count):
        at = pl.ds(start, count)
        for t in range(1, chips):
            k = lax.rem(me + rad - 2 * t, rad)
            remote(buf.at[k, at], buf.at[k, at], send_sem.at[g], far(part, t),
                   (h, core)).wait_recv()
            remote(buf.at[k, at], buf.at[k, at], send_sem.at[g], near_sem.at[near],
                   (h, core)).start()

    def gather_finish(g, near, buf, start, count):
        every = buf.at[pl.ds(0, chips), pl.ds(start, count)]
        remote(every, every, send_sem.at[g], near_sem.at[near], (h, core)).wait_recv()

    def gather_sent(g, buf):
        every = buf.at[pl.ds(0, rad - 1)]
        remote(every, every, send_sem.at[g], near_sem.at[0], (h, core)).wait_send()

    def raw_part(start, count):
        at = pl.ds(start, count)
        return remote(own.at[:, at, pl.ds(0, pair)], don01.at[:, at, :],
                      don_sem.at[0], don_sem.at[1], (across, me))

    head = max(rdev // 8, 16)
    applied = remote(vbuf, don23, don_sem.at[0], don_sem.at[2], (across, me))
    gather_start(0, 0, 0, gat_u, field.at[:, :, pl.ds(half, pair)], 0, elem)
    load_field.wait()
    raw_part(0, head).start()
    rim = nf * 3 * SIDE
    row_a, col_a = iota((rim, width), 0), iota((rim, width), 1)

    def across_lanes(place, u):
        return lax.dot_general(place, u, (((1,), (1,)), ((), ())), preferred_element_type=F32)

    def pack_rim(above, near_elem, far_elem):
        near = onehot(rim_position(col_a, node, SIDE, above, False) == row_a)
        far = onehot(rim_position(col_a, node, SIDE, above, True) == row_a)
        return (across_lanes(near, ext[near_elem]) + across_lanes(far, ext[far_elem])).astype(BF)

    pack[0] = pack_rim(False, HALO + elem - 1, HALO + elem - 2)
    pack[1] = pack_rim(True, HALO, HALO + 1)
    remote(pack.at[0], got.at[0], rim_sem.at[0], rim_sem.at[1], (up, me)).start()
    rim_down = remote(pack.at[1], got.at[1], rim_sem.at[0], rim_sem.at[1], (down, me))

    @pl.when(h != 0)
    def _():
        rim_down.start()


    @pl.when(inner)
    def _():
        raw_part(head, rdev - head).start()

    for cp in load_small:
        cp.wait()
    tile_t = onehot(iota((width, node), 0) % node == iota((width, node), 1))
    tile = onehot(iota((node, width), 1) % node == iota((node, width), 0))
    lrow, lcol = iota((width, width), 0), iota((width, width), 1)
    same = lrow // node == lcol // node

    def spread(block, tt, t, keep):
        return jnp.where(keep, dot(dot(tt, block).astype(BF), t), 0.0).astype(BF)

    both = deriv[...]
    grad_w[:, 0 * width:1 * width] = spread(both[:, :node], tile_t, tile, same)
    grad_w[:, 1 * width:2 * width] = spread(both[:, node:], tile_t, tile, same)
    match = lrow % node == lcol % node
    grad_w[:, 2 * width:3 * width] = onehot(match & (lrow // node == 0))
    grad_w[:, 3 * width:4 * width] = onehot(match & (lrow // node == 1))
    face_t = dot(face[...], tile).astype(BF)
    flane, fcol = iota((width, 4 * SIDE), 0) % node, iota((width, 4 * SIDE), 1)
    fi, fj, fq = flane // SIDE, flane % SIDE, fcol % SIDE
    for s in range(4):
        fixed, free = (fi, fj) if s < 2 else (fj, fi)
        at = SIDE - 1 if s % 2 == 0 else 0
        pick = onehot((fcol // SIDE == s) & (fixed == at) & (free == fq))
        face_w[s] = jnp.where(same, dot(pick, face_t), 0.0).astype(BF)
    ptile_t = onehot(iota((pair, node), 0) % node == iota((pair, node), 1))
    ptile = onehot(iota((node, pair), 1) % node == iota((node, pair), 0))
    psame = iota((pair, pair), 0) // node == iota((pair, pair), 1) // node
    for m in range(nmat):
        blocks[m] = spread(interp[m], ptile_t, ptile, psame)

    @pl.when((h == 0) & (second == 1))
    def _():
        pl.semaphore_wait(barrier, 3)
        pl.semaphore_signal(ready, inc=1, device_id=(h, core), device_id_type=MESH)

    @pl.when((h == 0) & (second == 0))
    def _():
        pl.semaphore_wait(ready, 1)

    @pl.when(h == 0)
    def _():
        rim_down.start()

    gat_u[me] = own[:, :, half:]
    inside = list(range(HALO, elem - HALO))
    listed = inside + [e for e in range(elem) if e not in inside]

    def local_stage(slot):
        e = listed[slot]
        u = ext[HALO + e]
        g = dot(u, grad_w[...])
        flux = g[:, 2 * width:3 * width] * g[:, :width] + g[:, 3 * width:] * g[:, width:2 * width]
        total = -flux
        for s in range(4):
            at = lax.rem(nbr[s, e] - first + HALO + elements, elements)
            at = jnp.minimum(at, elem + 2 * HALO - 1)
            total = total + dot(ext[at], face_w[s])
        gat_s[me, slot] = total[:, half:].astype(BF)
        local01[e] = total[:, :pair] + u[:, :pair].astype(F32)

    cuts = ((0, len(inside)), (len(inside), elem - len(inside)))

    def send_cut(c):
        start, count = cuts[c]
        gather_start(1, 1 + c, 1, gat_s, gat_s.at[me, pl.ds(start, count)], start, count)

    for slot in range(*cuts[0]):
        local_stage(slot)

    @pl.when(outer)
    def _():
        raw_part(head, rdev - head).start()

    lane = iota((rdev, 2 * pair), 1) % pair

    def radial_apply(which, buf, e):
        both_rows = rows[2 * which:2 * which + 2].reshape(2 * rdev, order)
        cols = jnp.concatenate(
            [buf[:, e].reshape(order, pair), buf[:, e + 1].reshape(order, pair)], axis=1
        )
        y = dot(both_rows, cols)
        return jnp.where(lane < node, y[:rdev], y[rdev:])

    gather_relay(0, 0, 0, gat_u, 0, elem)
    send_cut(0)
    gather_finish(0, 0, gat_u, 0, elem)
    load_rows.wait()
    for e in range(0, elem, 2):
        v = radial_apply(1, gat_u, e)
        for k in range(2):
            part = v[:, k * pair:(k + 1) * pair]
            acc23[e + k] = part
            vbuf[e + k] = part.astype(BF)

    remote(pack, got, rim_sem.at[0], rim_sem.at[1], (up, me)).wait_recv()

    def unpack(side, above, far):
        place = onehot(rim_position(col_a, node, SIDE, above, far) == row_a)
        return lax.dot_general(got[side], place, (((0,), (0,)), ((), ())),
                               preferred_element_type=F32).astype(BF)

    ext[0] = unpack(0, False, True)
    ext[1] = unpack(0, False, False)
    ext[HALO + elem] = unpack(1, True, False)
    ext[HALO + elem + 1] = unpack(1, True, True)

    for slot in range(cuts[1][0], elem):
        local_stage(slot)
    send_cut(1)

    def donors(src, e):
        total = None
        for d in range(ndon):
            at = lax.rem(don_id[d, e] - first - elements // 2 + 2 * elements, elements)
            at = jnp.minimum(at, elem - 1)
            term = dot(src[at], blocks[don_mat[d, e]])
            total = term if total is None else total + term
        return total

    remote(don01, don01, don_sem.at[0], don_sem.at[1], (across, me)).wait_recv()

    @pl.when(inner)
    def _():
        applied.start()

    parts = 2
    step = elem // parts
    for c in range(parts):
        for e in range(c * step, (c + 1) * step):
            gat_a[me, e] = (local01[e] + donors(don01, e)).astype(BF)
        gather_start(2, 3 + c, 2 + c, gat_a, gat_a.at[me, pl.ds(c * step, step)], c * step, step)

    for c, (start, count) in enumerate(cuts):
        gather_relay(1, 1 + c, 1, gat_s, start, count)
    gather_finish(1, 1, gat_s, 0, elem)
    for slot in range(0, elem, 2):
        v = radial_apply(1, gat_s, slot)
        for k in range(2):
            acc23[listed[slot + k]] += v[:, k * pair:(k + 1) * pair]


    @pl.when(outer)
    def _():
        applied.start()

    for c in range(parts):
        gather_relay(2, 3 + c, 2 + c, gat_a, c * step, step)
    def finish_applied():
        applied.wait_recv()
        for e in range(elem):
            out[e, :, half:] = (acc23[e] + donors(don23, e)).astype(BF)

    @pl.when(jnp.logical_not(last))
    def _():
        finish_applied()

    for c in range(parts):
        gather_finish(2, 2 + c, gat_a, c * step, step)
        for e in range(c * step, (c + 1) * step, 2):
            v = radial_apply(0, gat_a, e).astype(BF)
            for k in range(2):
                out[e + k, :, 0:pair] = v[:, k * pair:(k + 1) * pair]

    @pl.when(last)
    def _():
        finish_applied()

    for g, buf in enumerate((gat_u, gat_s, gat_a)):
        gather_sent(g, buf)
    remote(pack, got, rim_sem.at[0], rim_sem.at[1], (up, me)).wait_send()
    twice = gat_u.at[pl.ds(0, 2)]
    remote(twice, twice, don_sem.at[0], don_sem.at[1], (across, me)).wait_send()


def on_device(field_state, deriv_pair, face_blocks, interp_blocks, radial_ops,
              neighbours, donor_ids, donor_mats):
    elem, rdev, width = field_state.shape
    node = deriv_pair.shape[0]
    nf = width // node
    horiz, rad = lax.axis_size("horiz"), lax.axis_size("rad")
    nmat, ndon = interp_blocks.shape[0], donor_ids.shape[1]
    order, pair = rad * rdev, 2 * node
    dims = (horiz, rad, elem, rdev, nf, node, nmat, ndon)
    anyspec = pl.BlockSpec(memory_space=pl.ANY)
    vspec = pl.BlockSpec(memory_space=pltpu.VMEM)
    dma = pltpu.SemaphoreType.DMA
    return pl.pallas_call(
        functools.partial(kernel, dims),
        out_shape=pltpu.VMEM(field_state.shape, field_state.dtype),
        in_specs=[anyspec] * 8,
        out_specs=vspec,
        scratch_shapes=[
            pltpu.VMEM((elem + 2 * HALO, rdev, width), BF),
            pltpu.VMEM((nf, rdev, order), BF),
            pltpu.VMEM((2, nf * 3 * SIDE, rdev), BF),
            pltpu.VMEM((2, nf * 3 * SIDE, rdev), BF),
            pltpu.VMEM((width, 4 * width), BF),
            pltpu.VMEM((4, width, width), BF),
            pltpu.VMEM((nmat, pair, pair), BF),
            pltpu.VMEM((rad, elem, rdev, pair), BF),
            pltpu.VMEM((rad, elem, rdev, pair), BF),
            pltpu.VMEM((rad, elem, rdev, pair), BF),
            pltpu.VMEM((elem, rdev, pair), F32),
            pltpu.VMEM((elem, rdev, pair), F32),
            pltpu.VMEM((elem, rdev, pair), BF),
            pltpu.VMEM((elem, rdev, pair), BF),
            pltpu.VMEM((elem, rdev, pair), BF),
            pltpu.SMEM(neighbours.shape[::-1], jnp.int32),
            pltpu.SMEM(donor_ids.shape[::-1], jnp.int32),
            pltpu.SMEM(donor_mats.shape[::-1], jnp.int32),
            pltpu.VMEM(deriv_pair.shape, BF),
            pltpu.VMEM(face_blocks.shape, BF),
            pltpu.VMEM(interp_blocks.shape, BF),
            dma((8,)),
            dma((2,)),
            dma((3,)),
            dma((3,)),
            dma((5 * (rad // 2 - 1),)),
            dma((4,)),
            pltpu.SemaphoreType.REGULAR,
        ],
        compiler_params=pltpu.CompilerParams(collective_id=0, has_side_effects=True, vmem_limit_bytes=57000 * 1024),
    )(field_state, deriv_pair, face_blocks, interp_blocks, radial_ops,
      neighbours.T, donor_ids.T, donor_mats.T)


def solution(mesh):
    in_specs = (
        P("horiz", "rad", None), P(), P(), P(), P(),
        P("horiz", None), P("horiz", None), P("horiz", None),
    )
    return jax.shard_map(
        on_device, mesh=mesh, in_specs=in_specs, out_specs=P("horiz", "rad", None),
        check_vma=False,
    )
```

```python
import functools

import jax
import jax.numpy as jnp
from jax import lax
from jax.experimental import pallas as pl
from jax.experimental.pallas import tpu as pltpu
from jax.sharding import PartitionSpec as P

SIDE = 8
HALO = 2
MESH = pl.DeviceIdType.MESH
BF = jnp.bfloat16
F32 = jnp.float32


def dot(a, b):
    return jnp.dot(a, b, preferred_element_type=F32)


def iota(shape, dim):
    return lax.broadcasted_iota(jnp.int32, shape, dim)


def onehot(mask):
    return jnp.where(mask, 1.0, 0.0).astype(BF)


def rim_position(lane, node, side, above, far):
    field, n = lane // node, lane % node
    i, j = n // side, n % side
    last = 0 if above else side - 1
    base = field * (3 * side)
    if far:
        return jnp.where(j == last, base + 2 * side + i, -1)
    return jnp.where(i == last, base + j, jnp.where(j == last, base + side + i, -1))


def kernel(
    dims,
    field, deriv_in, face_in, interp_in, radial, nbr_in, don_id_in, don_mat_in,
    out,
    ext, rows, pack, got, grad_w, face_w, blocks,
    gat_u, gat_s, gat_a, local01, acc23, vbuf, don01, don23,
    nbr, don_id, don_mat, deriv, face, interp,
    local_sem, rim_sem, don_sem, send_sem, far_sem, near_sem, ready,
):
    horiz, rad, elem, rdev, nf, node, nmat, ndon = dims
    width = nf * node
    pair = 2 * node
    half = width - pair
    order = rad * rdev
    chips = rad // 2
    h, me = lax.axis_index("horiz"), lax.axis_index("rad")
    elements = elem * horiz
    first = h * elem
    up, down = lax.rem(h + 1, horiz), lax.rem(h + horiz - 1, horiz)
    across = lax.rem(h + horiz // 2, horiz)
    second = lax.rem(me, 2)
    core = me + 1 - 2 * second
    base = me - second
    quarter = horiz // 4
    outer = h >= horiz - quarter
    inner = jnp.logical_not(outer)
    last = ((h >= quarter) & (h < 2 * quarter)) | outer
    own = ext.at[pl.ds(HALO, elem)]

    barrier = pltpu.get_barrier_semaphore()
    peers = [
        (across, jnp.where(across == 0, base, me)),
        (up, jnp.where(up == 0, base + 1, me)),
        (down, jnp.where(down == 0, base, me)),
        (h, core),
    ]
    peers += [(h, lax.rem(jnp.where(h == 0, base, me) + 2 * t, rad)) for t in range(1, chips)]
    for peer in peers:
        pl.semaphore_signal(barrier, inc=1, device_id=peer, device_id_type=MESH)

    load_field = pltpu.make_async_copy(field, own, local_sem.at[0])
    load_rows = pltpu.make_async_copy(
        radial.at[:, pl.ds(pl.multiple_of(me * rdev, rdev), rdev), :], rows, local_sem.at[1]
    )
    load_field.start()
    load_small = [pltpu.make_async_copy(a, b, local_sem.at[2 + i]) for i, (a, b) in enumerate(
        ((deriv_in, deriv), (face_in, face), (interp_in, interp),
         (nbr_in, nbr), (don_id_in, don_id), (don_mat_in, don_mat)))]
    for cp in load_small:
        cp.start()
    load_rows.start()

    @pl.when(h != 0)
    def _():
        pl.semaphore_wait(barrier, len(peers))

    @pl.when((h == 0) & (second == 0))
    def _():
        pl.semaphore_wait(barrier, 2 * chips + 3)
        pl.semaphore_signal(ready, inc=1, device_id=(h, core), device_id_type=MESH)

    @pl.when((h == 0) & (second == 1))
    def _():
        pl.semaphore_wait(ready, 1)

    def remote(src, dst, send, recv, dev):
        return pltpu.make_async_remote_copy(
            src_ref=src, dst_ref=dst, send_sem=send, recv_sem=recv,
            device_id=dev, device_id_type=MESH,
        )

    def far(part, t):
        return far_sem.at[part * (chips - 1) + t - 1]

    def gather_start(g, part, near, buf, src, start, count):
        at = pl.ds(start, count)
        for t in range(1, chips):
            remote(src, buf.at[me, at], send_sem.at[g], far(part, t),
                   (h, lax.rem(me + 2 * t, rad))).start()
        remote(src, buf.at[me, at], send_sem.at[g], near_sem.at[near], (h, core)).start()

    def gather_relay(g, part, near, buf, start, count):
        at = pl.ds(start, count)
        for t in range(1, chips):
            k = lax.rem(me + rad - 2 * t, rad)
            remote(buf.at[k, at], buf.at[k, at], send_sem.at[g], far(part, t),
                   (h, core)).wait_recv()
            remote(buf.at[k, at], buf.at[k, at], send_sem.at[g], near_sem.at[near],
                   (h, core)).start()

    def gather_finish(g, near, buf, start, count):
        every = buf.at[pl.ds(0, chips), pl.ds(start, count)]
        remote(every, every, send_sem.at[g], near_sem.at[near], (h, core)).wait_recv()

    def gather_sent(g, buf):
        every = buf.at[pl.ds(0, rad - 1)]
        remote(every, every, send_sem.at[g], near_sem.at[0], (h, core)).wait_send()

    def raw_part(start, count):
        at = pl.ds(start, count)
        return remote(own.at[:, at, pl.ds(0, pair)], don01.at[:, at, :],
                      don_sem.at[0], don_sem.at[1], (across, me))

    head = max(rdev // 8, 16)
    piece = rdev // 2
    applied = [remote(vbuf.at[:, pl.ds(c * piece, piece), :], don23[c],
                      don_sem.at[0], don_sem.at[2 + c], (across, me)) for c in range(2)]
    gather_start(0, 0, 0, gat_u, field.at[:, :, pl.ds(half, pair)], 0, elem)
    load_field.wait()
    raw_part(0, head).start()
    rim = nf * 3 * SIDE
    row_a, col_a = iota((rim, width), 0), iota((rim, width), 1)

    def across_lanes(place, u):
        return lax.dot_general(place, u, (((1,), (1,)), ((), ())), preferred_element_type=F32)

    def pack_rim(above, near_elem, far_elem):
        near = onehot(rim_position(col_a, node, SIDE, above, False) == row_a)
        far = onehot(rim_position(col_a, node, SIDE, above, True) == row_a)
        return (across_lanes(near, ext[near_elem]) + across_lanes(far, ext[far_elem])).astype(BF)

    pack[0] = pack_rim(False, HALO + elem - 1, HALO + elem - 2)
    pack[1] = pack_rim(True, HALO, HALO + 1)
    remote(pack.at[0], got.at[0], rim_sem.at[0], rim_sem.at[1], (up, me)).start()
    rim_down = remote(pack.at[1], got.at[1], rim_sem.at[0], rim_sem.at[1], (down, me))

    @pl.when(h != 0)
    def _():
        rim_down.start()


    @pl.when(inner)
    def _():
        raw_part(head, rdev - head).start()

    for cp in load_small:
        cp.wait()
    tile_t = onehot(iota((width, node), 0) % node == iota((width, node), 1))
    tile = onehot(iota((node, width), 1) % node == iota((node, width), 0))
    lrow, lcol = iota((width, width), 0), iota((width, width), 1)
    same = lrow // node == lcol // node

    def spread(block, tt, t, keep):
        return jnp.where(keep, dot(dot(tt, block).astype(BF), t), 0.0).astype(BF)

    both = deriv[...]
    grad_w[:, 0 * width:1 * width] = spread(both[:, :node], tile_t, tile, same)
    grad_w[:, 1 * width:2 * width] = spread(both[:, node:], tile_t, tile, same)
    match = lrow % node == lcol % node
    grad_w[:, 2 * width:3 * width] = onehot(match & (lrow // node == 0))
    grad_w[:, 3 * width:4 * width] = onehot(match & (lrow // node == 1))
    face_t = dot(face[...], tile).astype(BF)
    flane, fcol = iota((width, 4 * SIDE), 0) % node, iota((width, 4 * SIDE), 1)
    fi, fj, fq = flane // SIDE, flane % SIDE, fcol % SIDE
    for s in range(4):
        fixed, free = (fi, fj) if s < 2 else (fj, fi)
        at = SIDE - 1 if s % 2 == 0 else 0
        pick = onehot((fcol // SIDE == s) & (fixed == at) & (free == fq))
        face_w[s] = jnp.where(same, dot(pick, face_t), 0.0).astype(BF)
    ptile_t = onehot(iota((pair, node), 0) % node == iota((pair, node), 1))
    ptile = onehot(iota((node, pair), 1) % node == iota((node, pair), 0))
    psame = iota((pair, pair), 0) // node == iota((pair, pair), 1) // node
    for m in range(nmat):
        blocks[m] = spread(interp[m], ptile_t, ptile, psame)

    @pl.when((h == 0) & (second == 1))
    def _():
        pl.semaphore_wait(barrier, 3)
        pl.semaphore_signal(ready, inc=1, device_id=(h, core), device_id_type=MESH)

    @pl.when((h == 0) & (second == 0))
    def _():
        pl.semaphore_wait(ready, 1)

    @pl.when(h == 0)
    def _():
        rim_down.start()

    gat_u[me] = own[:, :, half:]
    inside = list(range(HALO, elem - HALO))
    listed = inside + [e for e in range(elem) if e not in inside]

    def local_stage(slot):
        e = listed[slot]
        u = ext[HALO + e]
        g = dot(u, grad_w[...])
        flux = g[:, 2 * width:3 * width] * g[:, :width] + g[:, 3 * width:] * g[:, width:2 * width]
        total = -flux
        for s in range(4):
            at = lax.rem(nbr[s, e] - first + HALO + elements, elements)
            at = jnp.minimum(at, elem + 2 * HALO - 1)
            total = total + dot(ext[at], face_w[s])
        gat_s[me, slot] = total[:, half:].astype(BF)
        local01[e] = total[:, :pair] + u[:, :pair].astype(F32)

    cuts = ((0, len(inside)), (len(inside), elem - len(inside)))

    def send_cut(c):
        start, count = cuts[c]
        gather_start(1, 1 + c, 1, gat_s, gat_s.at[me, pl.ds(start, count)], start, count)

    for slot in range(*cuts[0]):
        local_stage(slot)

    @pl.when(outer)
    def _():
        raw_part(head, rdev - head).start()

    lane = iota((rdev, 2 * pair), 1) % pair

    def radial_apply(which, buf, e):
        both_rows = rows[2 * which:2 * which + 2].reshape(2 * rdev, order)
        cols = jnp.concatenate(
            [buf[:, e].reshape(order, pair), buf[:, e + 1].reshape(order, pair)], axis=1
        )
        y = dot(both_rows, cols)
        return jnp.where(lane < node, y[:rdev], y[rdev:])

    gather_relay(0, 0, 0, gat_u, 0, elem)
    send_cut(0)
    gather_finish(0, 0, gat_u, 0, elem)
    load_rows.wait()
    for e in range(0, elem, 2):
        v = radial_apply(1, gat_u, e)
        for k in range(2):
            part = v[:, k * pair:(k + 1) * pair]
            acc23[e + k] = part
            vbuf[e + k] = part.astype(BF)

    remote(pack, got, rim_sem.at[0], rim_sem.at[1], (up, me)).wait_recv()

    def unpack(side, above, far):
        place = onehot(rim_position(col_a, node, SIDE, above, far) == row_a)
        return lax.dot_general(got[side], place, (((0,), (0,)), ((), ())),
                               preferred_element_type=F32).astype(BF)

    ext[0] = unpack(0, False, True)
    ext[1] = unpack(0, False, False)
    ext[HALO + elem] = unpack(1, True, False)
    ext[HALO + elem + 1] = unpack(1, True, True)

    for slot in range(cuts[1][0], elem):
        local_stage(slot)
    send_cut(1)

    def donors(src, e):
        total = None
        for d in range(ndon):
            at = lax.rem(don_id[d, e] - first - elements // 2 + 2 * elements, elements)
            at = jnp.minimum(at, elem - 1)
            term = dot(src[at], blocks[don_mat[d, e]])
            total = term if total is None else total + term
        return total

    remote(don01, don01, don_sem.at[0], don_sem.at[1], (across, me)).wait_recv()

    @pl.when(inner & jnp.logical_not((second == 1) & (h >= horiz // 2) & inner))
    def _():
        for cp in applied:
            cp.start()

    parts = 2
    step = elem // parts
    for c in range(parts):
        for e in range(c * step, (c + 1) * step):
            gat_a[me, e] = (local01[e] + donors(don01, e)).astype(BF)
        gather_start(2, 3 + c, 2 + c, gat_a, gat_a.at[me, pl.ds(c * step, step)], c * step, step)


    @pl.when((second == 1) & (h >= horiz // 2) & inner)
    def _():
        for cp in applied:
            cp.start()

    for c, (start, count) in enumerate(cuts):
        gather_relay(1, 1 + c, 1, gat_s, start, count)
    gather_finish(1, 1, gat_s, 0, elem)
    for slot in range(0, elem, 2):
        v = radial_apply(1, gat_s, slot)
        for k in range(2):
            acc23[listed[slot + k]] += v[:, k * pair:(k + 1) * pair]


    @pl.when(outer)
    def _():
        for cp in applied:
            cp.start()

    for c in range(parts):
        gather_relay(2, 3 + c, 2 + c, gat_a, c * step, step)
    def finish_applied():
        for c, cp in enumerate(applied):
            cp.wait_recv()
            at = pl.ds(c * piece, piece)
            for e in range(elem):
                out[e, at, half:] = (acc23[e, at] + donors(don23[c], e)).astype(BF)

    @pl.when(jnp.logical_not(last))
    def _():
        finish_applied()

    for c in range(parts):
        gather_finish(2, 2 + c, gat_a, c * step, step)
        for e in range(c * step, (c + 1) * step, 2):
            v = radial_apply(0, gat_a, e).astype(BF)
            for k in range(2):
                out[e + k, :, 0:pair] = v[:, k * pair:(k + 1) * pair]

    @pl.when(last)
    def _():
        finish_applied()

    for g, buf in enumerate((gat_u, gat_s, gat_a)):
        gather_sent(g, buf)
    remote(pack, got, rim_sem.at[0], rim_sem.at[1], (up, me)).wait_send()
    twice = gat_u.at[pl.ds(0, 2)]
    remote(twice, twice, don_sem.at[0], don_sem.at[1], (across, me)).wait_send()


def on_device(field_state, deriv_pair, face_blocks, interp_blocks, radial_ops,
              neighbours, donor_ids, donor_mats):
    elem, rdev, width = field_state.shape
    node = deriv_pair.shape[0]
    nf = width // node
    horiz, rad = lax.axis_size("horiz"), lax.axis_size("rad")
    nmat, ndon = interp_blocks.shape[0], donor_ids.shape[1]
    order, pair = rad * rdev, 2 * node
    dims = (horiz, rad, elem, rdev, nf, node, nmat, ndon)
    anyspec = pl.BlockSpec(memory_space=pl.ANY)
    vspec = pl.BlockSpec(memory_space=pltpu.VMEM)
    dma = pltpu.SemaphoreType.DMA
    return pl.pallas_call(
        functools.partial(kernel, dims),
        out_shape=pltpu.VMEM(field_state.shape, field_state.dtype),
        in_specs=[anyspec] * 8,
        out_specs=vspec,
        scratch_shapes=[
            pltpu.VMEM((elem + 2 * HALO, rdev, width), BF),
            pltpu.VMEM((nf, rdev, order), BF),
            pltpu.VMEM((2, nf * 3 * SIDE, rdev), BF),
            pltpu.VMEM((2, nf * 3 * SIDE, rdev), BF),
            pltpu.VMEM((width, 4 * width), BF),
            pltpu.VMEM((4, width, width), BF),
            pltpu.VMEM((nmat, pair, pair), BF),
            pltpu.VMEM((rad, elem, rdev, pair), BF),
            pltpu.VMEM((rad, elem, rdev, pair), BF),
            pltpu.VMEM((rad, elem, rdev, pair), BF),
            pltpu.VMEM((elem, rdev, pair), F32),
            pltpu.VMEM((elem, rdev, pair), F32),
            pltpu.VMEM((elem, rdev, pair), BF),
            pltpu.VMEM((elem, rdev, pair), BF),
            [pltpu.VMEM((elem, rdev // 2, pair), BF) for _ in range(2)],
            pltpu.SMEM(neighbours.shape[::-1], jnp.int32),
            pltpu.SMEM(donor_ids.shape[::-1], jnp.int32),
            pltpu.SMEM(donor_mats.shape[::-1], jnp.int32),
            pltpu.VMEM(deriv_pair.shape, BF),
            pltpu.VMEM(face_blocks.shape, BF),
            pltpu.VMEM(interp_blocks.shape, BF),
            dma((8,)),
            dma((2,)),
            dma((4,)),
            dma((3,)),
            dma((5 * (rad // 2 - 1),)),
            dma((4,)),
            pltpu.SemaphoreType.REGULAR,
        ],
        compiler_params=pltpu.CompilerParams(collective_id=0, has_side_effects=True, vmem_limit_bytes=57000 * 1024),
    )(field_state, deriv_pair, face_blocks, interp_blocks, radial_ops,
      neighbours.T, donor_ids.T, donor_mats.T)


def solution(mesh):
    in_specs = (
        P("horiz", "rad", None), P(), P(), P(), P(),
        P("horiz", None), P("horiz", None), P("horiz", None),
    )
    return jax.shard_map(
        on_device, mesh=mesh, in_specs=in_specs, out_specs=P("horiz", "rad", None),
        check_vma=False,
    )
```

```python
import functools

import jax
import jax.numpy as jnp
from jax import lax
from jax.experimental import pallas as pl
from jax.experimental.pallas import tpu as pltpu
from jax.sharding import PartitionSpec as P

SIDE = 8
HALO = 2
MESH = pl.DeviceIdType.MESH
BF = jnp.bfloat16
F32 = jnp.float32


def dot(a, b):
    return jnp.dot(a, b, preferred_element_type=F32)


def iota(shape, dim):
    return lax.broadcasted_iota(jnp.int32, shape, dim)


def onehot(mask):
    return jnp.where(mask, 1.0, 0.0).astype(BF)


def rim_position(lane, node, side, above, far):
    field, n = lane // node, lane % node
    i, j = n // side, n % side
    last = 0 if above else side - 1
    base = field * (3 * side)
    if far:
        return jnp.where(j == last, base + 2 * side + i, -1)
    return jnp.where(i == last, base + j, jnp.where(j == last, base + side + i, -1))


def kernel(
    dims,
    field, deriv_in, face_in, interp_in, radial, nbr_in, don_id_in, don_mat_in,
    out,
    ext, rows, pack, got, grad_w, face_w, blocks,
    gathered, local01, acc23, vbuf, don01, don23,
    nbr, don_id, don_mat, deriv, face, interp,
    local_sem, rim_sem, don_sem, send_sem, far_sem, near_sem, ready,
):
    horiz, rad, elem, rdev, nf, node, nmat, ndon = dims
    width = nf * node
    pair = 2 * node
    half = width - pair
    order = rad * rdev
    chips = rad // 2
    h, me = lax.axis_index("horiz"), lax.axis_index("rad")
    elements = elem * horiz
    first = h * elem
    up, down = lax.rem(h + 1, horiz), lax.rem(h + horiz - 1, horiz)
    across = lax.rem(h + horiz // 2, horiz)
    second = lax.rem(me, 2)
    core = me + 1 - 2 * second
    base = me - second
    quarter = horiz // 4
    outer = h >= horiz - quarter
    inner = jnp.logical_not(outer)
    last = ((h >= quarter) & (h < 2 * quarter)) | outer
    own = ext.at[pl.ds(HALO, elem)]
    gat_u, gat_s, gat_a = [gathered.at[pl.ds(g * rad, rad)] for g in range(3)]

    load_field = pltpu.make_async_copy(field, own, local_sem.at[0])
    load_rows = pltpu.make_async_copy(
        radial.at[:, pl.ds(pl.multiple_of(me * rdev, rdev), rdev), :], rows, local_sem.at[1]
    )
    load_field.start()
    load_small = [pltpu.make_async_copy(a, b, local_sem.at[2 + i]) for i, (a, b) in enumerate(
        ((deriv_in, deriv), (face_in, face), (interp_in, interp),
         (nbr_in, nbr), (don_id_in, don_id), (don_mat_in, don_mat)))]
    for cp in load_small:
        cp.start()
    load_rows.start()

    barrier = pltpu.get_barrier_semaphore()
    peers = [
        (across, jnp.where(across == 0, base, me)),
        (up, jnp.where(up == 0, base + 1, me)),
        (down, jnp.where(down == 0, base, me)),
        (h, core),
    ]
    peers += [(h, lax.rem(jnp.where(h == 0, base, me) + 2 * t, rad)) for t in range(1, chips)]
    for peer in peers:
        pl.semaphore_signal(barrier, inc=1, device_id=peer, device_id_type=MESH)

    @pl.when(h != 0)
    def _():
        pl.semaphore_wait(barrier, len(peers))

    @pl.when((h == 0) & (second == 0))
    def _():
        pl.semaphore_wait(barrier, 2 * chips + 3)
        pl.semaphore_signal(ready, inc=1, device_id=(h, core), device_id_type=MESH)

    @pl.when((h == 0) & (second == 1))
    def _():
        pl.semaphore_wait(ready, 1)

    def remote(src, dst, send, recv, dev):
        return pltpu.make_async_remote_copy(
            src_ref=src, dst_ref=dst, send_sem=send, recv_sem=recv,
            device_id=dev, device_id_type=MESH,
        )

    def far(part, t):
        return far_sem.at[part * (chips - 1) + t - 1]

    def gather_start(g, part, near, buf, src, start, count):
        at = pl.ds(start, count)
        for t in range(1, chips):
            remote(src, buf.at[me, at], send_sem.at[0], far(part, t),
                   (h, lax.rem(me + 2 * t, rad))).start()
        remote(src, buf.at[me, at], send_sem.at[0], near_sem.at[near], (h, core)).start()

    def gather_relay(g, part, near, buf, start, count):
        at = pl.ds(start, count)
        for t in range(1, chips):
            k = lax.rem(me + rad - 2 * t, rad)
            remote(buf.at[k, at], buf.at[k, at], send_sem.at[0], far(part, t),
                   (h, core)).wait_recv()
            remote(buf.at[k, at], buf.at[k, at], send_sem.at[0], near_sem.at[near],
                   (h, core)).start()

    def gather_finish(g, near, buf, start, count):
        every = buf.at[pl.ds(0, chips), pl.ds(start, count)]
        remote(every, every, send_sem.at[0], near_sem.at[near], (h, core)).wait_recv()

    def raw_part(start, count):
        at = pl.ds(start, count)
        return remote(own.at[:, at, pl.ds(0, pair)], don01.at[:, at, :],
                      send_sem.at[0], don_sem.at[0], (across, me))

    head = max(rdev // 8, 16)
    applied = remote(vbuf, don23, send_sem.at[0], don_sem.at[1], (across, me))
    gather_start(0, 0, 0, gat_u, field.at[:, :, pl.ds(half, pair)], 0, elem)
    load_field.wait()
    raw_part(0, head).start()
    rim = nf * 3 * SIDE
    row_a, col_a = iota((rim, width), 0), iota((rim, width), 1)

    def across_lanes(place, u):
        return lax.dot_general(place, u, (((1,), (1,)), ((), ())), preferred_element_type=F32)

    def pack_rim(above, near_elem, far_elem):
        near = onehot(rim_position(col_a, node, SIDE, above, False) == row_a)
        far = onehot(rim_position(col_a, node, SIDE, above, True) == row_a)
        return (across_lanes(near, ext[near_elem]) + across_lanes(far, ext[far_elem])).astype(BF)

    pack[0] = pack_rim(False, HALO + elem - 1, HALO + elem - 2)
    pack[1] = pack_rim(True, HALO, HALO + 1)
    remote(pack.at[0], got.at[0], rim_sem.at[0], rim_sem.at[1], (up, me)).start()
    rim_down = remote(pack.at[1], got.at[1], rim_sem.at[0], rim_sem.at[1], (down, me))

    @pl.when(h != 0)
    def _():
        rim_down.start()


    @pl.when(inner)
    def _():
        raw_part(head, rdev - head).start()

    for cp in load_small:
        cp.wait()
    tile_t = onehot(iota((width, node), 0) % node == iota((width, node), 1))
    tile = onehot(iota((node, width), 1) % node == iota((node, width), 0))
    lrow, lcol = iota((width, width), 0), iota((width, width), 1)
    same = lrow // node == lcol // node

    def spread(block, tt, t, keep):
        return jnp.where(keep, dot(dot(tt, block).astype(BF), t), 0.0).astype(BF)

    both = deriv[...]
    grad_w[:, 0 * width:1 * width] = spread(both[:, :node], tile_t, tile, same)
    grad_w[:, 1 * width:2 * width] = spread(both[:, node:], tile_t, tile, same)
    match = lrow % node == lcol % node
    grad_w[:, 2 * width:3 * width] = onehot(match & (lrow // node == 0))
    grad_w[:, 3 * width:4 * width] = onehot(match & (lrow // node == 1))
    face_t = dot(face[...], tile).astype(BF)
    flane, fcol = iota((width, 4 * SIDE), 0) % node, iota((width, 4 * SIDE), 1)
    fi, fj, fq = flane // SIDE, flane % SIDE, fcol % SIDE
    for s in range(4):
        fixed, free = (fi, fj) if s < 2 else (fj, fi)
        at = SIDE - 1 if s % 2 == 0 else 0
        pick = onehot((fcol // SIDE == s) & (fixed == at) & (free == fq))
        face_w[s] = jnp.where(same, dot(pick, face_t), 0.0).astype(BF)
    ptile_t = onehot(iota((pair, node), 0) % node == iota((pair, node), 1))
    ptile = onehot(iota((node, pair), 1) % node == iota((node, pair), 0))
    psame = iota((pair, pair), 0) // node == iota((pair, pair), 1) // node
    for m in range(nmat):
        blocks[m] = spread(interp[m], ptile_t, ptile, psame)

    @pl.when((h == 0) & (second == 1))
    def _():
        pl.semaphore_wait(barrier, 3)
        pl.semaphore_signal(ready, inc=1, device_id=(h, core), device_id_type=MESH)

    @pl.when((h == 0) & (second == 0))
    def _():
        pl.semaphore_wait(ready, 1)

    @pl.when(h == 0)
    def _():
        rim_down.start()

    gat_u[me] = own[:, :, half:]
    inside = list(range(HALO, elem - HALO))
    listed = inside + [e for e in range(elem) if e not in inside]

    def local_stage(slot):
        e = listed[slot]
        u = ext[HALO + e]
        g = dot(u, grad_w[...])
        flux = g[:, 2 * width:3 * width] * g[:, :width] + g[:, 3 * width:] * g[:, width:2 * width]
        total = -flux
        for s in range(4):
            at = lax.rem(nbr[s, e] - first + HALO + elements, elements)
            at = jnp.minimum(at, elem + 2 * HALO - 1)
            total = total + dot(ext[at], face_w[s])
        gat_s[me, slot] = total[:, half:].astype(BF)
        local01[e] = total[:, :pair] + u[:, :pair].astype(F32)

    cuts = ((0, len(inside)), (len(inside), elem - len(inside)))

    def send_cut(c):
        start, count = cuts[c]
        gather_start(1, 1 + c, 1, gat_s, gat_s.at[me, pl.ds(start, count)], start, count)

    for slot in range(*cuts[0]):
        local_stage(slot)

    @pl.when(outer)
    def _():
        raw_part(head, rdev - head).start()

    lane = iota((rdev, 2 * pair), 1) % pair

    def radial_apply(which, buf, e):
        both_rows = rows[2 * which:2 * which + 2].reshape(2 * rdev, order)
        cols = jnp.concatenate(
            [buf[:, e].reshape(order, pair), buf[:, e + 1].reshape(order, pair)], axis=1
        )
        y = dot(both_rows, cols)
        return jnp.where(lane < node, y[:rdev], y[rdev:])

    gather_relay(0, 0, 0, gat_u, 0, elem)
    send_cut(0)
    gather_finish(0, 0, gat_u, 0, elem)
    load_rows.wait()
    for e in range(0, elem, 2):
        v = radial_apply(1, gat_u, e)
        for k in range(2):
            part = v[:, k * pair:(k + 1) * pair]
            acc23[e + k] = part
            vbuf[e + k] = part.astype(BF)

    remote(pack, got, rim_sem.at[0], rim_sem.at[1], (up, me)).wait_recv()

    def unpack(side, above, far):
        place = onehot(rim_position(col_a, node, SIDE, above, far) == row_a)
        return lax.dot_general(got[side], place, (((0,), (0,)), ((), ())),
                               preferred_element_type=F32).astype(BF)

    ext[0] = unpack(0, False, True)
    ext[1] = unpack(0, False, False)
    ext[HALO + elem] = unpack(1, True, False)
    ext[HALO + elem + 1] = unpack(1, True, True)

    for slot in range(cuts[1][0], elem):
        local_stage(slot)
    send_cut(1)

    def donors(src, e):
        total = None
        for d in range(ndon):
            at = lax.rem(don_id[d, e] - first - elements // 2 + 2 * elements, elements)
            at = jnp.minimum(at, elem - 1)
            term = dot(src[at], blocks[don_mat[d, e]])
            total = term if total is None else total + term
        return total

    remote(don01, don01, send_sem.at[0], don_sem.at[0], (across, me)).wait_recv()

    @pl.when(inner)
    def _():
        applied.start()

    parts = 2
    step = elem // parts
    for c in range(parts):
        for e in range(c * step, (c + 1) * step):
            gat_a[me, e] = (local01[e] + donors(don01, e)).astype(BF)
        gather_start(2, 3 + c, 2 + c, gat_a, gat_a.at[me, pl.ds(c * step, step)], c * step, step)

    for c, (start, count) in enumerate(cuts):
        gather_relay(1, 1 + c, 1, gat_s, start, count)
    gather_finish(1, 1, gat_s, 0, elem)
    for slot in range(0, elem, 2):
        v = radial_apply(1, gat_s, slot)
        for k in range(2):
            acc23[listed[slot + k]] += v[:, k * pair:(k + 1) * pair]


    @pl.when(outer)
    def _():
        applied.start()

    for c in range(parts):
        gather_relay(2, 3 + c, 2 + c, gat_a, c * step, step)
    def finish_applied():
        applied.wait_recv()
        for e in range(elem):
            out[e, :, half:] = (acc23[e] + donors(don23, e)).astype(BF)

    @pl.when(jnp.logical_not(last))
    def _():
        finish_applied()

    for c in range(parts):
        gather_finish(2, 2 + c, gat_a, c * step, step)
        for e in range(c * step, (c + 1) * step, 2):
            v = radial_apply(0, gat_a, e).astype(BF)
            for k in range(2):
                out[e + k, :, 0:pair] = v[:, k * pair:(k + 1) * pair]

    @pl.when(last)
    def _():
        finish_applied()

    remote(pack, got, rim_sem.at[0], rim_sem.at[1], (up, me)).wait_send()
    every = gathered.at[pl.ds(0, 3 * (rad - 1) + 2)]
    remote(every, every, send_sem.at[0], don_sem.at[0], (across, me)).wait_send()


def on_device(field_state, deriv_pair, face_blocks, interp_blocks, radial_ops,
              neighbours, donor_ids, donor_mats):
    elem, rdev, width = field_state.shape
    node = deriv_pair.shape[0]
    nf = width // node
    horiz, rad = lax.axis_size("horiz"), lax.axis_size("rad")
    nmat, ndon = interp_blocks.shape[0], donor_ids.shape[1]
    order, pair = rad * rdev, 2 * node
    dims = (horiz, rad, elem, rdev, nf, node, nmat, ndon)
    anyspec = pl.BlockSpec(memory_space=pl.ANY)
    vspec = pl.BlockSpec(memory_space=pltpu.VMEM)
    dma = pltpu.SemaphoreType.DMA
    return pl.pallas_call(
        functools.partial(kernel, dims),
        out_shape=pltpu.VMEM(field_state.shape, field_state.dtype),
        in_specs=[anyspec] * 8,
        out_specs=vspec,
        scratch_shapes=[
            pltpu.VMEM((elem + 2 * HALO, rdev, width), BF),
            pltpu.VMEM((nf, rdev, order), BF),
            pltpu.VMEM((2, nf * 3 * SIDE, rdev), BF),
            pltpu.VMEM((2, nf * 3 * SIDE, rdev), BF),
            pltpu.VMEM((width, 4 * width), BF),
            pltpu.VMEM((4, width, width), BF),
            pltpu.VMEM((nmat, pair, pair), BF),
            pltpu.VMEM((3 * rad, elem, rdev, pair), BF),
            pltpu.VMEM((elem, rdev, pair), F32),
            pltpu.VMEM((elem, rdev, pair), F32),
            pltpu.VMEM((elem, rdev, pair), BF),
            pltpu.VMEM((elem, rdev, pair), BF),
            pltpu.VMEM((elem, rdev, pair), BF),
            pltpu.SMEM(neighbours.shape[::-1], jnp.int32),
            pltpu.SMEM(donor_ids.shape[::-1], jnp.int32),
            pltpu.SMEM(donor_mats.shape[::-1], jnp.int32),
            pltpu.VMEM(deriv_pair.shape, BF),
            pltpu.VMEM(face_blocks.shape, BF),
            pltpu.VMEM(interp_blocks.shape, BF),
            dma((8,)),
            dma((2,)),
            dma((2,)),
            dma((1,)),
            dma((5 * (rad // 2 - 1),)),
            dma((4,)),
            pltpu.SemaphoreType.REGULAR,
        ],
        compiler_params=pltpu.CompilerParams(collective_id=0, has_side_effects=True, vmem_limit_bytes=57000 * 1024),
    )(field_state, deriv_pair, face_blocks, interp_blocks, radial_ops,
      neighbours.T, donor_ids.T, donor_mats.T)


def solution(mesh):
    in_specs = (
        P("horiz", "rad", None), P(), P(), P(), P(),
        P("horiz", None), P("horiz", None), P("horiz", None),
    )
    return jax.shard_map(
        on_device, mesh=mesh, in_specs=in_specs, out_specs=P("horiz", "rad", None),
        check_vma=False,
    )
```

```python
import functools

import jax
import jax.numpy as jnp
from jax import lax
from jax.experimental import pallas as pl
from jax.experimental.pallas import tpu as pltpu
from jax.sharding import PartitionSpec as P

SIDE = 8
HALO = 2
MESH = pl.DeviceIdType.MESH
BF = jnp.bfloat16
F32 = jnp.float32


def dot(a, b):
    return jnp.dot(a, b, preferred_element_type=F32)


def iota(shape, dim):
    return lax.broadcasted_iota(jnp.int32, shape, dim)


def onehot(mask):
    return jnp.where(mask, 1.0, 0.0).astype(BF)


def rim_position(lane, node, side, above, far):
    field, n = lane // node, lane % node
    i, j = n // side, n % side
    last = 0 if above else side - 1
    base = field * (3 * side)
    if far:
        return jnp.where(j == last, base + 2 * side + i, -1)
    return jnp.where(i == last, base + j, jnp.where(j == last, base + side + i, -1))


def kernel(
    dims,
    field, deriv_in, face_in, interp_in, radial, nbr_in, don_id_in, don_mat_in,
    out,
    ext, rows, pack, got, grad_w, face_w, blocks,
    gat_u, gat_s, gat_a, local01, acc23, vbuf, don01, don23,
    nbr, don_id, don_mat, deriv, face, interp,
    local_sem, rim_sem, don_sem, send_sem, far_sem, near_sem, ready,
):
    horiz, rad, elem, rdev, nf, node, nmat, ndon = dims
    width = nf * node
    pair = 2 * node
    half = width - pair
    order = rad * rdev
    chips = rad // 2
    h, me = lax.axis_index("horiz"), lax.axis_index("rad")
    elements = elem * horiz
    first = h * elem
    up, down = lax.rem(h + 1, horiz), lax.rem(h + horiz - 1, horiz)
    across = lax.rem(h + horiz // 2, horiz)
    second = lax.rem(me, 2)
    core = me + 1 - 2 * second
    base = me - second
    quarter = horiz // 4
    outer = h >= horiz - quarter
    inner = jnp.logical_not(outer)
    last = ((h >= quarter) & (h < 2 * quarter)) | outer
    own = ext.at[pl.ds(HALO, elem)]

    load_field = pltpu.make_async_copy(field, own, local_sem.at[0])
    load_rows = pltpu.make_async_copy(
        radial.at[:, pl.ds(pl.multiple_of(me * rdev, rdev), rdev), :], rows, local_sem.at[1]
    )
    load_field.start()
    load_small = [pltpu.make_async_copy(a, b, local_sem.at[2 + i]) for i, (a, b) in enumerate(
        ((deriv_in, deriv), (face_in, face), (interp_in, interp),
         (nbr_in, nbr), (don_id_in, don_id), (don_mat_in, don_mat)))]
    for cp in load_small:
        cp.start()
    load_rows.start()

    barrier = pltpu.get_barrier_semaphore()
    peers = [
        (across, jnp.where(across == 0, base, me)),
        (up, jnp.where(up == 0, base + 1, me)),
        (down, jnp.where(down == 0, base, me)),
        (h, core),
    ]
    peers += [(h, lax.rem(jnp.where(h == 0, base, me) + 2 * t, rad)) for t in range(1, chips)]
    for peer in peers:
        pl.semaphore_signal(barrier, inc=1, device_id=peer, device_id_type=MESH)

    @pl.when(h != 0)
    def _():
        pl.semaphore_wait(barrier, len(peers))

    @pl.when((h == 0) & (second == 0))
    def _():
        pl.semaphore_wait(barrier, 2 * chips + 3)
        pl.semaphore_signal(ready, inc=1, device_id=(h, core), device_id_type=MESH)

    @pl.when((h == 0) & (second == 1))
    def _():
        pl.semaphore_wait(ready, 1)

    def remote(src, dst, send, recv, dev):
        return pltpu.make_async_remote_copy(
            src_ref=src, dst_ref=dst, send_sem=send, recv_sem=recv,
            device_id=dev, device_id_type=MESH,
        )

    def far(part, t):
        return far_sem.at[part * (chips - 1) + t - 1]

    def gather_start(g, part, near, buf, src, start, count):
        at = pl.ds(start, count)
        for t in range(1, chips):
            remote(src, buf.at[me, at], send_sem.at[g], far(part, t),
                   (h, lax.rem(me + 2 * t, rad))).start()
        remote(src, buf.at[me, at], send_sem.at[g], near_sem.at[near], (h, core)).start()

    def gather_relay(g, part, near, buf, start, count):
        at = pl.ds(start, count)
        for t in range(1, chips):
            k = lax.rem(me + rad - 2 * t, rad)
            remote(buf.at[k, at], buf.at[k, at], send_sem.at[g], far(part, t),
                   (h, core)).wait_recv()
            remote(buf.at[k, at], buf.at[k, at], send_sem.at[g], near_sem.at[near],
                   (h, core)).start()

    def gather_finish(g, near, buf, start, count):
        every = buf.at[pl.ds(0, chips), pl.ds(start, count)]
        remote(every, every, send_sem.at[g], near_sem.at[near], (h, core)).wait_recv()

    def gather_sent(g, buf):
        every = buf.at[pl.ds(0, rad - 1)]
        remote(every, every, send_sem.at[g], near_sem.at[0], (h, core)).wait_send()

    def raw_part(start, count):
        at = pl.ds(start, count)
        return remote(own.at[:, at, pl.ds(0, pair)], don01.at[:, at, :],
                      don_sem.at[0], don_sem.at[1], (across, me))

    head = max(rdev // 8, 16)
    applied = remote(vbuf, don23, don_sem.at[0], don_sem.at[2], (across, me))
    gather_start(0, 0, 0, gat_u, field.at[:, :, pl.ds(half, pair)], 0, elem)
    load_field.wait()
    raw_part(0, head).start()
    rim = nf * 3 * SIDE
    row_a, col_a = iota((rim, width), 0), iota((rim, width), 1)

    def across_lanes(place, u):
        return lax.dot_general(place, u, (((1,), (1,)), ((), ())), preferred_element_type=F32)

    def pack_rim(above, near_elem, far_elem):
        near = onehot(rim_position(col_a, node, SIDE, above, False) == row_a)
        far = onehot(rim_position(col_a, node, SIDE, above, True) == row_a)
        return (across_lanes(near, ext[near_elem]) + across_lanes(far, ext[far_elem])).astype(BF)

    pack[0] = pack_rim(False, HALO + elem - 1, HALO + elem - 2)
    pack[1] = pack_rim(True, HALO, HALO + 1)
    remote(pack.at[0], got.at[0], rim_sem.at[0], rim_sem.at[1], (up, me)).start()
    rim_down = remote(pack.at[1], got.at[1], rim_sem.at[0], rim_sem.at[1], (down, me))

    @pl.when(h != 0)
    def _():
        rim_down.start()


    @pl.when(inner)
    def _():
        raw_part(head, rdev - head).start()

    for cp in load_small:
        cp.wait()
    tile_t = onehot(iota((width, node), 0) % node == iota((width, node), 1))
    tile = onehot(iota((node, width), 1) % node == iota((node, width), 0))
    lrow, lcol = iota((width, width), 0), iota((width, width), 1)
    same = lrow // node == lcol // node

    def spread(block, tt, t, keep):
        return jnp.where(keep, dot(dot(tt, block).astype(BF), t), 0.0).astype(BF)

    both = deriv[...]
    grad_w[:, 0 * width:1 * width] = spread(both[:, :node], tile_t, tile, same)
    grad_w[:, 1 * width:2 * width] = spread(both[:, node:], tile_t, tile, same)
    match = lrow % node == lcol % node
    grad_w[:, 2 * width:3 * width] = onehot(match & (lrow // node == 0))
    grad_w[:, 3 * width:4 * width] = onehot(match & (lrow // node == 1))
    face_t = dot(face[...], tile).astype(BF)
    flane, fcol = iota((width, 4 * SIDE), 0) % node, iota((width, 4 * SIDE), 1)
    fi, fj, fq = flane // SIDE, flane % SIDE, fcol % SIDE
    for s in range(4):
        fixed, free = (fi, fj) if s < 2 else (fj, fi)
        at = SIDE - 1 if s % 2 == 0 else 0
        pick = onehot((fcol // SIDE == s) & (fixed == at) & (free == fq))
        face_w[s] = jnp.where(same, dot(pick, face_t), 0.0).astype(BF)
    ptile_t = onehot(iota((pair, node), 0) % node == iota((pair, node), 1))
    ptile = onehot(iota((node, pair), 1) % node == iota((node, pair), 0))
    psame = iota((pair, pair), 0) // node == iota((pair, pair), 1) // node
    for m in range(nmat):
        blocks[m] = spread(interp[m], ptile_t, ptile, psame)

    @pl.when((h == 0) & (second == 1))
    def _():
        pl.semaphore_wait(barrier, 3)
        pl.semaphore_signal(ready, inc=1, device_id=(h, core), device_id_type=MESH)

    @pl.when((h == 0) & (second == 0))
    def _():
        pl.semaphore_wait(ready, 1)

    @pl.when(h == 0)
    def _():
        rim_down.start()

    gat_u[me] = own[:, :, half:]
    inside = list(range(HALO, elem - HALO))
    listed = inside + [e for e in range(elem) if e not in inside]

    def local_stage(slot):
        e = listed[slot]
        u = ext[HALO + e]
        g = dot(u, grad_w[...])
        flux = g[:, 2 * width:3 * width] * g[:, :width] + g[:, 3 * width:] * g[:, width:2 * width]
        total = -flux
        for s in range(4):
            at = lax.rem(nbr[s, e] - first + HALO + elements, elements)
            at = jnp.minimum(at, elem + 2 * HALO - 1)
            total = total + dot(ext[at], face_w[s])
        gat_s[me, slot] = total[:, half:].astype(BF)
        local01[e] = total[:, :pair] + u[:, :pair].astype(F32)

    cuts = ((0, len(inside)), (len(inside), elem - len(inside)))

    def send_cut(c):
        start, count = cuts[c]
        gather_start(1, 1 + c, 1, gat_s, gat_s.at[me, pl.ds(start, count)], start, count)

    for slot in range(*cuts[0]):
        local_stage(slot)

    @pl.when(outer)
    def _():
        raw_part(head, rdev - head).start()

    lane = iota((rdev, 2 * pair), 1) % pair

    def radial_apply(which, buf, e):
        both_rows = rows[2 * which:2 * which + 2].reshape(2 * rdev, order)
        cols = jnp.concatenate(
            [buf[:, e].reshape(order, pair), buf[:, e + 1].reshape(order, pair)], axis=1
        )
        y = dot(both_rows, cols)
        return jnp.where(lane < node, y[:rdev], y[rdev:])

    gather_relay(0, 0, 0, gat_u, 0, elem)
    send_cut(0)
    gather_finish(0, 0, gat_u, 0, elem)
    load_rows.wait()
    for e in range(0, elem, 2):
        v = radial_apply(1, gat_u, e)
        for k in range(2):
            part = v[:, k * pair:(k + 1) * pair]
            acc23[e + k] = part
            vbuf[e + k] = part.astype(BF)


    @pl.when((h >= quarter) & inner)
    def _():
        applied.start()

    remote(pack, got, rim_sem.at[0], rim_sem.at[1], (up, me)).wait_recv()

    def unpack(side, above, far):
        place = onehot(rim_position(col_a, node, SIDE, above, far) == row_a)
        return lax.dot_general(got[side], place, (((0,), (0,)), ((), ())),
                               preferred_element_type=F32).astype(BF)

    ext[0] = unpack(0, False, True)
    ext[1] = unpack(0, False, False)
    ext[HALO + elem] = unpack(1, True, False)
    ext[HALO + elem + 1] = unpack(1, True, True)

    for slot in range(cuts[1][0], elem):
        local_stage(slot)
    send_cut(1)

    def donors(src, e):
        total = None
        for d in range(ndon):
            at = lax.rem(don_id[d, e] - first - elements // 2 + 2 * elements, elements)
            at = jnp.minimum(at, elem - 1)
            term = dot(src[at], blocks[don_mat[d, e]])
            total = term if total is None else total + term
        return total

    remote(don01, don01, don_sem.at[0], don_sem.at[1], (across, me)).wait_recv()

    @pl.when(h < quarter)
    def _():
        applied.start()

    parts = 2
    step = elem // parts
    for c in range(parts):
        for e in range(c * step, (c + 1) * step):
            gat_a[me, e] = (local01[e] + donors(don01, e)).astype(BF)
        gather_start(2, 3 + c, 2 + c, gat_a, gat_a.at[me, pl.ds(c * step, step)], c * step, step)

    for c, (start, count) in enumerate(cuts):
        gather_relay(1, 1 + c, 1, gat_s, start, count)
    gather_finish(1, 1, gat_s, 0, elem)
    for slot in range(0, elem, 2):
        v = radial_apply(1, gat_s, slot)
        for k in range(2):
            acc23[listed[slot + k]] += v[:, k * pair:(k + 1) * pair]


    @pl.when(outer)
    def _():
        applied.start()

    for c in range(parts):
        gather_relay(2, 3 + c, 2 + c, gat_a, c * step, step)
    def finish_applied():
        applied.wait_recv()
        for e in range(elem):
            out[e, :, half:] = (acc23[e] + donors(don23, e)).astype(BF)

    @pl.when(jnp.logical_not(last))
    def _():
        finish_applied()

    for c in range(parts):
        gather_finish(2, 2 + c, gat_a, c * step, step)
        for e in range(c * step, (c + 1) * step, 2):
            v = radial_apply(0, gat_a, e).astype(BF)
            for k in range(2):
                out[e + k, :, 0:pair] = v[:, k * pair:(k + 1) * pair]

    @pl.when(last)
    def _():
        finish_applied()

    for g, buf in enumerate((gat_u, gat_s, gat_a)):
        gather_sent(g, buf)
    remote(pack, got, rim_sem.at[0], rim_sem.at[1], (up, me)).wait_send()
    twice = gat_u.at[pl.ds(0, 2)]
    remote(twice, twice, don_sem.at[0], don_sem.at[1], (across, me)).wait_send()


def on_device(field_state, deriv_pair, face_blocks, interp_blocks, radial_ops,
              neighbours, donor_ids, donor_mats):
    elem, rdev, width = field_state.shape
    node = deriv_pair.shape[0]
    nf = width // node
    horiz, rad = lax.axis_size("horiz"), lax.axis_size("rad")
    nmat, ndon = interp_blocks.shape[0], donor_ids.shape[1]
    order, pair = rad * rdev, 2 * node
    dims = (horiz, rad, elem, rdev, nf, node, nmat, ndon)
    anyspec = pl.BlockSpec(memory_space=pl.ANY)
    vspec = pl.BlockSpec(memory_space=pltpu.VMEM)
    dma = pltpu.SemaphoreType.DMA
    return pl.pallas_call(
        functools.partial(kernel, dims),
        out_shape=pltpu.VMEM(field_state.shape, field_state.dtype),
        in_specs=[anyspec] * 8,
        out_specs=vspec,
        scratch_shapes=[
            pltpu.VMEM((elem + 2 * HALO, rdev, width), BF),
            pltpu.VMEM((nf, rdev, order), BF),
            pltpu.VMEM((2, nf * 3 * SIDE, rdev), BF),
            pltpu.VMEM((2, nf * 3 * SIDE, rdev), BF),
            pltpu.VMEM((width, 4 * width), BF),
            pltpu.VMEM((4, width, width), BF),
            pltpu.VMEM((nmat, pair, pair), BF),
            pltpu.VMEM((rad, elem, rdev, pair), BF),
            pltpu.VMEM((rad, elem, rdev, pair), BF),
            pltpu.VMEM((rad, elem, rdev, pair), BF),
            pltpu.VMEM((elem, rdev, pair), F32),
            pltpu.VMEM((elem, rdev, pair), F32),
            pltpu.VMEM((elem, rdev, pair), BF),
            pltpu.VMEM((elem, rdev, pair), BF),
            pltpu.VMEM((elem, rdev, pair), BF),
            pltpu.SMEM(neighbours.shape[::-1], jnp.int32),
            pltpu.SMEM(donor_ids.shape[::-1], jnp.int32),
            pltpu.SMEM(donor_mats.shape[::-1], jnp.int32),
            pltpu.VMEM(deriv_pair.shape, BF),
            pltpu.VMEM(face_blocks.shape, BF),
            pltpu.VMEM(interp_blocks.shape, BF),
            dma((8,)),
            dma((2,)),
            dma((3,)),
            dma((3,)),
            dma((5 * (rad // 2 - 1),)),
            dma((4,)),
            pltpu.SemaphoreType.REGULAR,
        ],
        compiler_params=pltpu.CompilerParams(collective_id=0, has_side_effects=True, vmem_limit_bytes=57000 * 1024),
    )(field_state, deriv_pair, face_blocks, interp_blocks, radial_ops,
      neighbours.T, donor_ids.T, donor_mats.T)


def solution(mesh):
    in_specs = (
        P("horiz", "rad", None), P(), P(), P(), P(),
        P("horiz", None), P("horiz", None), P("horiz", None),
    )
    return jax.shard_map(
        on_device, mesh=mesh, in_specs=in_specs, out_specs=P("horiz", "rad", None),
        check_vma=False,
    )
```
